128 devices in a mesh: prow: 8 (over x_lo, y), pcol: 16 (over x_hi, z, core).
Axes of the slice: x: 4 (x_hi: 2, x_lo: 2; x = x_hi * 2 + x_lo), y: 4, z: 4, core: 2. Of those that a mesh axis runs over, the one named last changes fastest.
Arguments:
- window: float32 [20480, 20480], P('prow', 'pcol'), as said below
- pattern: int32 [160, 160], P('prow', 'pcol'), may hold values from 0 to 1, as said below
- row_lists: int32 [2, 2, 64], replicated, may hold values from 0 to 159, as said below
- factor: float32 [2, 20480, 256], P(None, 'prow', 'pcol'), may hold values from -0.5 to 0.5
- diag_inverse: float32 [2, 128, 256], replicated, as said below
Outputs:
- panels: float32 [2, 20480, 256], P(None, 'pcol', 'prow')
- diagonals: float32 [2, 128, 256], P(None, None, 'prow')
The draws below stay inside these ranges and needn't reach their ends.
Inputs may be any that keep to these rules, and one draw needn't show every extreme that they name: `pattern`: Symmetric; every diagonal block is stored; about 85 in 100 blocks are stored. `row_lists`: each list names distinct blocks. The lists of level 0 never name blocks 160 - 2 and 159; list s of level 1 is the first 62 entries of list s of level 0 followed by 160 - 2 and 159. `window`: exactly symmetric. `diag_inverse`: each of the two 128 x 128 blocks of a level is symmetric up to rounding.
All inputs are finite; a program needn't handle non-finite values.
Results may differ from the reference program's by a relative error of at most 0.00011.
Values sent between devices are 32-bit elements; how exact they have to be, the bound alone decides.
A program may use at most 128 MiB of HBM per device.

```python
import jax
import jax.numpy as jnp
from jax import lax

BS = 128
NB = 160
RS = 64
ROWS = 20480


def draw_window(key, part):
    total_rows = NB * BS
    base = jax.random.normal(key, (total_rows, total_rows), jnp.float32)
    symmetric = (base + base.T) * 0.70710678
    return symmetric * (0.85 * RS) ** (-0.5)


def draw_pattern(key, part):
    numbers = jax.random.randint(key, (NB, NB), 0, 100)
    stored = (numbers < 85).astype(jnp.int32)
    symmetric = jnp.triu(stored) + jnp.triu(stored, 1).T
    return jnp.maximum(symmetric, jnp.eye(NB, dtype=jnp.int32)).astype(jnp.int32)


def draw_row_lists(key, part):
    first_level = []
    second_level = []
    for node_index in range(2):
        subkey = jax.random.fold_in(key, 11 + node_index)
        shuffled = jax.random.permutation(subkey, NB - 2).astype(jnp.int32)
        listed = shuffled[:RS]
        first_level.append(listed)
        second_level.append(jnp.concatenate([listed[:RS - 2], jnp.array([NB - 2, NB - 1], dtype=jnp.int32)]))
    return jnp.stack([jnp.stack(first_level), jnp.stack(second_level)]).astype(jnp.int32)


def draw_diag_inverse(key, part):
    base = 2.0 * jax.random.normal(key, (2, 2, BS, BS), jnp.float32)
    symmetric = (base + jnp.swapaxes(base, 2, 3)) * 0.70710678
    return jnp.concatenate([symmetric[:, 0], symmetric[:, 1]], axis=2)


def levels(own_key, dims, pieces, least, largest):
    loudness = 1.0
    for axis_at, parts in pieces:
        draws = jax.random.uniform(jax.random.fold_in(jax.random.fold_in(own_key, 6), axis_at), (parts,), jnp.float32, least / len(pieces), largest / len(pieces))
        loudness = loudness * jnp.repeat(jnp.exp(draws), dims[axis_at] // parts).reshape((-1,) + (1,) * (len(dims) - 1 - axis_at))
    return loudness


def noise(own_key, extent, scale, reach, cuts=(), kind=jnp.bfloat16):
    drawn = jax.random.normal(own_key, extent, jnp.float32) * scale
    if len(cuts) > 0:
        drawn = levels(own_key, extent, cuts, -0.22, 0.18) * drawn
    return jnp.clip(drawn, min=-reach, max=reach).astype(kind)


def setup_inputs(seed: int = 0) -> dict:
    seeds = jax.random.split(jax.random.key(seed), 6)
    window = draw_window(jax.random.fold_in(seeds[5], 71), 0)
    pattern = draw_pattern(jax.random.fold_in(seeds[5], 71), 0)
    row_lists = draw_row_lists(jax.random.fold_in(seeds[5], 71), 0)
    factor = noise(seeds[3], (2, ROWS, 2 * BS), BS ** -0.5, 0.5, ((1, 8), (2, 16)), jnp.float32)
    diag_inverse = draw_diag_inverse(jax.random.fold_in(seeds[5], 71), 0)
    return dict(window=window, pattern=pattern, row_lists=row_lists, factor=factor, diag_inverse=diag_inverse)


exact_mode = lax.Precision.HIGHEST


def block_flags(index_lists):
    blocks = jnp.arange(NB, dtype=jnp.int32)
    return jnp.any(blocks[None, :, None] == index_lists[:, None, :], axis=-1).astype(jnp.float32)


def cell_mask(index_lists):
    flags = jnp.repeat(block_flags(index_lists), BS, axis=1)
    first_half = jnp.broadcast_to(flags[0][:, None], (NB * BS, BS))
    second_half = jnp.broadcast_to(flags[1][:, None], (NB * BS, BS))
    return jnp.concatenate([first_half, second_half], axis=1)


def window_product(window, pattern, factor_panel):
    blocks = jnp.arange(NB, dtype=jnp.int32)
    usable = (blocks < NB - 2).astype(jnp.float32)
    keeper = pattern.astype(jnp.float32) * usable[:, None] * usable[None, :]
    strips = window.reshape(NB, BS, NB * BS)

    def one_strip(inputs):
        strip_rows, keep_row = inputs
        masked = (strip_rows.reshape(BS, NB, BS) * keep_row[None, :, None]).reshape(BS, NB * BS)
        return jnp.dot(masked, factor_panel, precision=exact_mode, preferred_element_type=jnp.float32)

    return lax.map(one_strip, (strips, keeper)).reshape(NB * BS, 2 * BS)


def diag_block(live_factor, solved, inverse_part):
    gram_first = jnp.dot(live_factor[:, :BS].T, solved[:, :BS], precision=exact_mode, preferred_element_type=jnp.float32)
    gram_second = jnp.dot(live_factor[:, BS:].T, solved[:, BS:], precision=exact_mode, preferred_element_type=jnp.float32)
    return inverse_part - jnp.concatenate([gram_first, gram_second], axis=1)


def reference(window, pattern, row_lists, factor, diag_inverse):
    total_rows = NB * BS
    mask_one = cell_mask(row_lists[0])
    live_one = factor[0] * mask_one
    image_one = window_product(window, pattern, live_one)
    solved_one = -(mask_one * image_one)
    diag_one = diag_block(live_one, solved_one, diag_inverse[0])
    mask_two = cell_mask(row_lists[1])
    live_two = factor[1] * mask_two
    image_two = window_product(window, pattern, live_two)
    slot_rows = live_two[total_rows - 2 * BS:]
    image_two = image_two + jnp.dot(solved_one, slot_rows, precision=exact_mode, preferred_element_type=jnp.float32)
    corner = jnp.dot(solved_one.T, live_two, precision=exact_mode, preferred_element_type=jnp.float32)
    corner = corner + jnp.concatenate([
        jnp.dot(diag_one[:, :BS], slot_rows[:BS], precision=exact_mode, preferred_element_type=jnp.float32),
        jnp.dot(diag_one[:, BS:], slot_rows[BS:], precision=exact_mode, preferred_element_type=jnp.float32)], axis=0)
    image_two = jnp.concatenate([image_two[:total_rows - 2 * BS], image_two[total_rows - 2 * BS:] + corner], axis=0)
    solved_two = -(mask_two * image_two)
    diag_two = diag_block(live_two, solved_two, diag_inverse[1])
    return jnp.stack([solved_one, solved_two]), jnp.stack([diag_one, diag_two])
```

```python
import jax
import jax.numpy as jnp
from jax import lax
from jax.experimental import pallas as pl
from jax.experimental.pallas import tpu as pltpu
from jax.sharding import PartitionSpec as P

BS = 128
NB = 160
RB = 20
CB = 10
ROWS = RB * BS
COLS = CB * BS
SMALL = 512
LANES = 2 * COLS + SMALL
MESH = pl.DeviceIdType.MESH
F32 = jnp.float32
BF16 = jnp.bfloat16


def remote(src, dst, send, recv, device):
    return pltpu.make_async_remote_copy(
        src_ref=src, dst_ref=dst, send_sem=send, recv_sem=recv, device_id=device, device_id_type=MESH
    )


def coords():
    r = lax.axis_index("prow")
    c = lax.axis_index("pcol")
    return r, c, r // 4, r % 4, c // 8, (c // 2) % 4, c % 2


class PairRing:
    def __init__(self, send, recv, block, half, device, p, y, sent):
        self.s, self.r, self.block, self.half, self.device = send, recv, block, half, device
        self.p, self.y, self.sent = p, y, sent
        self.q = 1 - p
        self.right, self.left, self.far = (y + 1) % 4, (y + 3) % 4, (y + 2) % 4

    def push(self, k, src, dst, device):
        copy = remote(src, dst, self.s.at[k], self.r.at[k], device)
        copy.start()
        self.sent.append(copy)

    def wait(self, k, ref):
        remote(ref, ref, self.s.at[k], self.r.at[k], self.device(self.p, self.right)).wait_recv()

    def start(self, src):
        own = self.block(self.p, self.y)
        self.push(0, src, own, self.device(self.q, self.y))
        self.push(1, src, own, self.device(self.p, self.right))
        self.push(2, src, own, self.device(self.p, self.left))

    def from_left(self, own):
        k, p = (1, self.p) if own else (5, self.q)
        self.wait(k, self.block(p, self.left))
        part = self.half(p, self.left, 0)
        self.push(k + 2, part, part, self.device(self.p, self.right))

    def from_right(self, own):
        k, p = (2, self.p) if own else (6, self.q)
        self.wait(k, self.block(p, self.right))
        part = self.half(p, self.right, 1)
        self.push(k + 2, part, part, self.device(self.p, self.left))

    def from_pair(self):
        other = self.block(self.q, self.y)
        self.wait(0, other)
        self.push(5, other, other, self.device(self.p, self.right))
        self.push(6, other, other, self.device(self.p, self.left))

    def from_far(self, own):
        k, p = (3, self.p) if own else (7, self.q)
        self.wait(k, self.half(p, self.far, 0))
        self.wait(k + 1, self.half(p, self.far, 1))


def gather_kernel(f_ref, fr_ref, fc_ref, q_ref, as_, ar, bs, br, cs, cr, ts, tr, qs, qr, ks, kr, local):
    r, c, xl, y, xh, z, k = coords()
    cc = c // 2
    other = c + 1 - 2 * k
    diagonal = r == cc
    barrier = pltpu.get_barrier_semaphore()

    def greet(device):
        pl.semaphore_signal(barrier, inc=1, device_id=device, device_id_type=MESH)

    for d in range(1, 8):
        greet((r, ((cc + d) % 8) * 2 + k))
        greet(((r + d) % 8, c))
    greet((r, other))

    @pl.when(jnp.logical_not(diagonal))
    def _():
        greet((cc, 2 * r))
        greet((cc, 2 * r + 1))
        pl.semaphore_wait(barrier, 17)

    @pl.when(diagonal)
    def _():
        pl.semaphore_wait(barrier, 15)

    sent = []
    ga = PairRing(
        as_, ar,
        lambda p, w: fr_ref.at[p * 8 + w * 2 + k],
        lambda p, w, h: fr_ref.at[p * 8 + w * 2 + k, h],
        lambda p, w: (r, p * 8 + w * 2 + k),
        xh, z, sent,
    )
    gb = PairRing(
        bs, br,
        lambda p, w: fc_ref.at[p * 4 + w],
        lambda p, w, h: fc_ref.at[p * 4 + w, h],
        lambda p, w: (p * 4 + w, c),
        xl, y, sent,
    )
    last = f_ref.at[1, :, pl.ds(ROWS - 2 * BS, 2 * BS)]
    own_q = q_ref.at[cc, k]

    @pl.when(r == 7)
    def _():
        copy = pltpu.make_async_copy(last, own_q, local.at[0])
        copy.start()
        for d in range(7):
            remote(last, own_q, qs.at[d], qr.at[0], (d, c)).start()

    ga.start(f_ref)
    own = pltpu.make_async_copy(f_ref, fr_ref.at[c], local.at[1])
    own.start()

    @pl.when(jnp.logical_not(diagonal))
    def _():
        for h in range(2):
            remote(
                f_ref.at[:, :, pl.ds(h * COLS, COLS)], fc_ref.at[cc, k], ts.at[h], tr.at[k], (cc, 2 * r + h)
            ).start()

    @pl.when(diagonal)
    def _():
        remote(
            f_ref.at[:, :, pl.ds((1 - k) * COLS, COLS)], fc_ref.at[cc, k], ts.at[0], tr.at[k], (r, other)
        ).start()
        pltpu.make_async_copy(f_ref.at[:, :, pl.ds(k * COLS, COLS)], fc_ref.at[r, k], local.at[2]).start()

    def swap(chip, src=None):
        block = fr_ref.at[chip * 2 + k]
        copy = remote(block if src is None else src, block, cs.at[chip], cr.at[chip], (r, other))
        copy.start()
        sent.append(copy)

    swap(cc, f_ref)

    @pl.when(r == 7)
    def _():
        pltpu.make_async_copy(last, own_q, local.at[0]).wait()

    @pl.when(r != 7)
    def _():
        remote(own_q, own_q, qs.at[0], qr.at[0], (r, other)).wait_recv()

    for d in range(1, 8):
        copy = remote(own_q, own_q, qs.at[7 + d], qr.at[d], (r, ((cc + d) % 8) * 2 + k))
        copy.start()
        sent.append(copy)

    chip = lambda p, w: p * 4 + w
    right, left, far = (z + 1) % 4, (z + 3) % 4, (z + 2) % 4
    mine = fc_ref.at[r]

    @pl.when(jnp.logical_not(diagonal))
    def _():
        for h in range(2):
            part = fc_ref.at[r, h]
            remote(part, part, ts.at[h], tr.at[h], (r, other)).wait_recv()

    @pl.when(diagonal)
    def _():
        part = fc_ref.at[r, 1 - k]
        remote(part, part, ts.at[0], tr.at[1 - k], (r, other)).wait_recv()
        pltpu.make_async_copy(f_ref.at[:, :, pl.ds(k * COLS, COLS)], fc_ref.at[r, k], local.at[2]).wait()

    gb.start(mine)
    ga.from_left(True)
    swap(chip(xh, left))
    ga.from_right(True)
    swap(chip(xh, right))
    ga.from_pair()
    swap(chip(1 - xh, z))
    gb.from_left(True)
    gb.from_right(True)
    gb.from_pair()
    ga.from_far(True)
    swap(chip(xh, far))
    for d in range(1, 8):
        part = q_ref.at[(cc + 8 - d) % 8, k]
        remote(part, part, qs.at[0], qr.at[d], (r, other)).wait_recv()
    half = q_ref.at[:, k]
    copy = remote(half, half, ks.at[0], kr.at[0], (r, other))
    copy.start()
    sent.append(copy)
    ga.from_left(False)
    swap(chip(1 - xh, left))
    ga.from_right(False)
    swap(chip(1 - xh, right))
    gb.from_far(True)
    gb.from_left(False)
    gb.from_right(False)
    ga.from_far(False)
    swap(chip(1 - xh, far))
    gb.from_far(False)
    for chip_index in range(8):
        block = fr_ref.at[chip_index * 2 + 1 - k]
        remote(block, block, cs.at[chip_index], cr.at[chip_index], (r, other)).wait_recv()
    half = q_ref.at[:, 1 - k]
    remote(half, half, ks.at[0], kr.at[0], (r, other)).wait_recv()
    own.wait()
    for copy in sent:
        copy.wait_send()

    @pl.when(r == 7)
    def _():
        for d in range(7):
            remote(last, own_q, qs.at[d], qr.at[0], (d, c)).wait_send()

    @pl.when(jnp.logical_not(diagonal))
    def _():
        for h in range(2):
            remote(
                f_ref.at[:, :, pl.ds(h * COLS, COLS)], fc_ref.at[cc, k], ts.at[h], tr.at[k], (cc, 2 * r + h)
            ).wait_send()

    @pl.when(diagonal)
    def _():
        remote(
            f_ref.at[:, :, pl.ds((1 - k) * COLS, COLS)], fc_ref.at[cc, k], ts.at[0], tr.at[k], (r, other)
        ).wait_send()


def split(x):
    hi = x.astype(BF16)
    return hi, (x - hi.astype(F32)).astype(BF16)


def dot3(a, b, nt=False):
    dims = (((1,), (1 if nt else 0,)), ((), ()))
    (ah, al), (bh, bl) = a, b
    one = lambda u, v: lax.dot_general(u, v, dims, preferred_element_type=F32)
    return one(ah, bh) + (one(ah, bl) + one(al, bh))


def product_kernel(
    rl, pat, w_ref, fr_ref, fc_ref, q_ref, d_ref, x_ref,
    wc, frc, fh, fl, x1, ch, cl, c0h, c0l, ph, pw, acc, rb, cb, rf, cf, wsem, fsem,
):
    r = lax.axis_index("prow")
    c = lax.axis_index("pcol")

    for s in range(2):
        for q in range(CB):
            cf[s, q] = 0

    def scan(p, carry):
        out = []
        for s in range(2):
            n, m = carry[2 * s], carry[2 * s + 1]
            b = rl[0, s, p]
            keep = jnp.where(p < 62, 1, 0)
            lr = b - r * RB
            lc = b - c * CB
            usable = b < NB - 2
            inr = jnp.logical_and(jnp.logical_and(lr >= 0, lr < RB), usable)
            inc = jnp.logical_and(jnp.logical_and(lc >= 0, lc < CB), usable)
            rb[s, n] = lr
            rf[s, n] = keep
            cb[s, m] = lc

            @pl.when(inc)
            def _():
                cf[s, lc] = keep

            out += [n + inr.astype(jnp.int32), m + inc.astype(jnp.int32)]
        return tuple(out)

    zero = jnp.int32(0)
    n0, m0, n1, m1 = lax.fori_loop(0, 64, scan, (zero, zero, zero, zero))
    counts = ((n0, m0), (n1, m1))

    @pl.when(c == 15)
    def _():
        for s in range(2):
            for q in (8, 9):
                cf[s, q] = 1

    def f_copy(s, i):
        return pltpu.make_async_copy(
            fr_ref.at[pl.ds(8 * s, 8), :, :, pl.ds(pl.multiple_of(rb[s, i] * BS, BS), BS)],
            frc.at[s, i], fsem.at[s, i],
        )

    def w_copy(s, i, j):
        return pltpu.make_async_copy(
            w_ref.at[pl.ds(pl.multiple_of(rb[s, i] * BS, BS), BS), pl.ds(pl.multiple_of(cb[s, j] * BS, BS), BS)],
            wc.at[s, pl.ds(pl.multiple_of(i * BS, BS), BS), pl.ds(pl.multiple_of(j * BS, BS), BS)],
            wsem.at[s, i, j],
        )

    for s in range(2):
        n, m = counts[s]

        @pl.loop(0, n)
        def _(i):
            f_copy(s, i).start()

            @pl.loop(0, m)
            def _(j):
                stored = pat[cb[s, j], rb[s, i]] != 0

                @pl.when(stored)
                def _():
                    w_copy(s, i, j).start()

                @pl.when(jnp.logical_not(stored))
                def _():
                    wc[s, pl.ds(pl.multiple_of(i * BS, BS), BS), pl.ds(pl.multiple_of(j * BS, BS), BS)] = jnp.zeros(
                        (BS, BS), F32
                    )

        @pl.when(n % 2 == 1)
        def _():
            frc[s, n] = jnp.zeros((8, 2, 16, BS), F32)
            wc[s, pl.ds(pl.multiple_of(n * BS, BS), BS), :] = jnp.zeros((BS, COLS), F32)

    x_ref[:, pl.ds(0, COLS)] = jnp.zeros((256, COLS), F32)
    x1[...] = jnp.zeros((256, COLS), F32)

    for s in range(2):
        for q in range(CB):
            lanes = pl.ds(q * BS, BS)
            rows = pl.ds(s * BS, BS)
            block = fc_ref[pl.ds(4 * s, 4), :, 1, :, lanes].reshape(BS, BS) * cf[s, q].astype(F32)
            ch[rows, lanes], cl[rows, lanes] = split(block)
            block = fc_ref[pl.ds(4 * s, 4), :, 0, :, lanes].reshape(BS, BS)
            c0h[rows, lanes], c0l[rows, lanes] = split(block)

    for s in range(2):
        n, m = counts[s]

        @pl.loop(0, n)
        def _(i):
            f_copy(s, i).wait()

        @pl.loop(0, (n + 1) // 2)
        def _(i):
            for t in range(2):
                keep = rf[s, 2 * i + t].astype(F32)
                for level in range(2):
                    block = frc[s, 2 * i + t, :, level].reshape(BS, BS)
                    if level == 1:
                        block = block * keep
                    hi, lo = split(block)
                    fh[i, pl.ds(level * BS, BS), pl.ds(t * BS, BS)] = hi
                    fl[i, pl.ds(level * BS, BS), pl.ds(t * BS, BS)] = lo

        @pl.loop(0, n)
        def _(i):
            @pl.loop(0, m)
            def _(j):
                @pl.when(pat[cb[s, j], rb[s, i]] != 0)
                def _():
                    w_copy(s, i, j).wait()

        @pl.loop(0, (m + 1) // 2)
        def _(j):
            acc[...] = jnp.zeros((256, 256), F32)

            @pl.loop(0, (n + 1) // 2)
            def _(i):
                block = wc[
                    s, pl.ds(pl.multiple_of(i * 256, 256), 256), pl.ds(pl.multiple_of(j * 256, 256), 256)
                ]
                acc[...] += dot3((fh[i], fl[i]), split(block))

            for t in range(2):
                @pl.when(2 * j + t < m)
                def _():
                    lanes = pl.ds(pl.multiple_of(cb[s, 2 * j + t] * BS, BS), BS)
                    x_ref[pl.ds(s * BS, BS), lanes] = -acc[pl.ds(0, BS), pl.ds(t * BS, BS)]
                    x1[pl.ds(s * BS, BS), lanes] = acc[pl.ds(BS, BS), pl.ds(t * BS, BS)]

    qv = split(q_ref[...].reshape(256, 256))
    ph[...], pw[...] = split(x_ref[:, pl.ds(0, COLS)])
    pair = lambda h, l, rows: (h[rows, :], l[rows, :])
    whole = pl.ds(0, 256)
    a_t = dot3(pair(ch, cl, whole), pair(ph, pw, whole), nt=True)
    chosen = jnp.where(jnp.logical_and(r == 0, c == 0), 1.0, 0.0).astype(F32)
    s_t = []
    for s in range(2):
        rows = pl.ds(s * BS, BS)
        s_t.append(chosen * d_ref[0, :, rows] - dot3(pair(ph, pw, rows), pair(c0h, c0l, rows), nt=True))
    slot = a_t + jnp.concatenate(
        [dot3((qv[0][:, s * BS:(s + 1) * BS], qv[1][:, s * BS:(s + 1) * BS]), split(s_t[s])) for s in range(2)], axis=1
    )
    a_s, slot_s = split(a_t), split(slot)
    base = 2 * COLS
    for s in range(2):
        rows = pl.ds(s * BS, BS)
        cut = lambda v: (v[0][s * BS:(s + 1) * BS], v[1][s * BS:(s + 1) * BS])
        second = (
            chosen * d_ref[1, :, rows]
            + dot3(split(x1[rows, :]), pair(ch, cl, rows), nt=True)
            + dot3(cut(qv), cut(a_s), nt=True)
            + dot3(cut(slot_s), cut(qv), nt=True)
        )
        x_ref[rows, pl.ds(base, BS)] = s_t[s]
        x_ref[rows, pl.ds(base + BS, BS)] = second
        x_ref[rows, pl.ds(base + 2 * BS, 2 * BS)] = -slot[s * BS:(s + 1) * BS]

    for q in range(0, CB, 2):
        lanes = pl.ds(q * BS, 2 * BS)
        full = x1[:, lanes] + dot3(qv, (ph[:, lanes], pw[:, lanes]))
        for s in range(2):
            for t in range(2):
                part = full[s * BS:(s + 1) * BS, t * BS:(t + 1) * BS]
                x_ref[pl.ds(s * BS, BS), pl.ds(COLS + (q + t) * BS, BS)] = -cf[s, q + t].astype(F32) * part


def reduce_kernel(
    x_ref, panels, diagonals, ax, asum, al, ar, aown, ahl, ahr, yl, yr, yhl, yhr, ysum, yx, fin,
    core, mine, parts, done, xs, xr, rs, rr, ss, sr, cs, cr,
):
    r, c, xl, y, xh, z, k = coords()
    cc = c // 2
    other = c + 1 - 2 * k
    px = (4 * (1 - xl) + y, c)
    right, left, far = (y + 1) % 4, (y + 3) % 4, (y + 2) % 4
    dr, dl = (4 * xl + right, c), (4 * xl + left, c)
    barrier = pltpu.get_barrier_semaphore()
    for device in [px, dr, dl, (r, other)] + [(r, ((cc + d) % 8) * 2 + k) for d in range(1, 8)]:
        pl.semaphore_signal(barrier, inc=1, device_id=device, device_id_type=MESH)
    pl.semaphore_wait(barrier, 11)
    sent = []

    def push(src, dst, send, recv, device):
        copy = remote(src, dst, send, recv, device)
        copy.start()
        sent.append(copy)

    def arrived(ref, send, recv):
        remote(ref, ref, send, recv, px).wait_recv()

    def rows(p, w, h=None):
        if h is None:
            return pl.ds(pl.multiple_of((4 * p + w) * 32, 32), 32)
        return pl.ds(pl.multiple_of((4 * p + w) * 32 + 16 * h, 16), 16)

    lane_a = pl.ds(0, COLS)
    streams = ((2 * COLS, SMALL), (COLS, COLS))

    def ring_first(t, p, v):
        start, width = streams[t]
        lanes = pl.ds(start, width)
        e = 2 * t + v
        push(x_ref.at[rows(p, far, 0), lanes], yhl[t].at[v], rs.at[e, 0], rr.at[e, 0], dr)
        push(x_ref.at[rows(p, far, 1), lanes], yhr[t].at[v], rs.at[e, 1], rr.at[e, 1], dl)

    def ring_second(t, p, v):
        start, width = streams[t]
        lanes = pl.ds(start, width)
        e = 2 * t + v
        arrived(yhl[t].at[v], rs.at[e, 0], rr.at[e, 0])
        low = x_ref[rows(p, right, 0), lanes] + yhl[t][v]
        ysum[t][v, 0, pl.ds(0, 16), :] = low
        ysum[t][v, 0, pl.ds(16, 16), :] = x_ref[rows(p, right, 1), lanes]
        push(ysum[t].at[v, 0], yl[t].at[v], rs.at[e, 2], rr.at[e, 2], dr)
        arrived(yhr[t].at[v], rs.at[e, 1], rr.at[e, 1])
        ysum[t][v, 1, pl.ds(0, 16), :] = x_ref[rows(p, left, 0), lanes]
        ysum[t][v, 1, pl.ds(16, 16), :] = x_ref[rows(p, left, 1), lanes] + yhr[t][v]
        push(ysum[t].at[v, 1], yr[t].at[v], rs.at[e, 3], rr.at[e, 3], dl)

    def ring_third(t, p, v):
        start, width = streams[t]
        e = 2 * t + v
        arrived(yl[t].at[v], rs.at[e, 2], rr.at[e, 2])
        arrived(yr[t].at[v], rs.at[e, 3], rr.at[e, 3])
        return x_ref[rows(p, y), pl.ds(start, width)] + (yl[t][v] + yr[t][v])

    q = 1 - xl
    ring_first(0, q, 0)
    ring_first(0, xl, 1)
    for w, d in ((0, far), (1, right), (2, left), (3, y)):
        push(x_ref.at[rows(q, d), lane_a], ax.at[w], xs.at[w], xr.at[w], px)
    ring_first(1, q, 0)
    ring_second(0, q, 0)
    ring_second(0, xl, 1)
    ring_first(1, xl, 1)
    ring_second(1, q, 0)

    fin[0][...] = ring_third(0, q, 0)
    push(fin[0], yx[0], xs.at[4], xr.at[4], px)
    ring_second(1, xl, 1)

    arrived(ax.at[0], xs.at[0], xr.at[0])
    asum[0] = x_ref[rows(xl, far), lane_a] + ax[0]
    push(asum.at[0, pl.ds(0, 16)], ahl, rs.at[4, 0], rr.at[4, 0], dr)
    push(asum.at[0, pl.ds(16, 16)], ahr, rs.at[4, 1], rr.at[4, 1], dl)

    small = ring_third(0, xl, 1)
    arrived(yx[0], xs.at[4], xr.at[4])
    mine[...] = small + yx[0][...]
    push(mine, core, cs.at[0], cr.at[0], (r, other))

    arrived(ax.at[1], xs.at[1], xr.at[1])
    asum[1] = x_ref[rows(xl, right), lane_a] + ax[1]
    arrived(ahl, rs.at[4, 0], rr.at[4, 0])
    asum[1, pl.ds(0, 16)] = asum[1, pl.ds(0, 16)] + ahl[...]
    push(asum.at[1], al, rs.at[4, 2], rr.at[4, 2], dr)

    arrived(core, cs.at[0], cr.at[0])
    own_half = pl.ds(pl.multiple_of(16 * k, 16), 16)
    parts[cc] = mine[own_half, :] + core[own_half, :]
    for d in range(1, 8):
        push(parts.at[cc], parts.at[cc], ss.at[d], sr.at[d], (r, ((cc + d) % 8) * 2 + k))

    arrived(ax.at[2], xs.at[2], xr.at[2])
    asum[2] = x_ref[rows(xl, left), lane_a] + ax[2]
    arrived(ahr, rs.at[4, 1], rr.at[4, 1])
    asum[2, pl.ds(16, 16)] = asum[2, pl.ds(16, 16)] + ahr[...]
    push(asum.at[2], ar, rs.at[4, 3], rr.at[4, 3], dl)

    fin[1][...] = ring_third(1, q, 0)
    push(fin[1], yx[1], xs.at[5], xr.at[5], px)

    for d in range(1, 8):
        arrived(parts.at[(cc + 8 - d) % 8], ss.at[d], sr.at[d])
    total = parts[0]
    for d in range(1, 8):
        total = total + parts[d]
    done[own_half, :] = total
    push(done.at[own_half], done.at[own_half], cs.at[1], cr.at[1], (r, other))

    arrived(ax.at[3], xs.at[3], xr.at[3])
    first = x_ref[rows(xl, y), lane_a] + ax[3]
    second = ring_third(1, xl, 1)
    arrived(al, rs.at[4, 2], rr.at[4, 2])
    arrived(ar, rs.at[4, 3], rr.at[4, 3])
    panels[0] = first + (al[...] + ar[...])
    arrived(yx[1], xs.at[5], xr.at[5])
    panels[1] = second + yx[1][...]
    other_half = pl.ds(pl.multiple_of(16 * (1 - k), 16), 16)
    arrived(done.at[other_half], cs.at[1], cr.at[1])
    diagonals[0] = done[:, pl.ds(0, BS)]
    diagonals[1] = done[:, pl.ds(BS, BS)]
    at_end = jnp.where(c == 15, 1.0, 0.0).astype(F32)
    tail = pl.ds(COLS - 2 * BS, 2 * BS)
    panels[1, :, tail] = panels[1, :, tail] + at_end * done[:, pl.ds(2 * BS, 2 * BS)]
    for copy in sent:
        copy.wait_send()


def local(window, pattern, row_lists, factor, diag_inverse):
    dma = pltpu.SemaphoreType.DMA
    hbm = pl.BlockSpec(memory_space=pl.ANY)
    vmem = pl.BlockSpec(memory_space=pltpu.VMEM)
    smem = pl.BlockSpec(memory_space=pltpu.SMEM)
    f_t = jnp.swapaxes(factor, 1, 2)
    fr, fc, q_t = pl.pallas_call(
        gather_kernel,
        out_shape=(
            jax.ShapeDtypeStruct((16, 2, 16, ROWS), F32),
            jax.ShapeDtypeStruct((8, 2, 2, 16, COLS), F32),
            jax.ShapeDtypeStruct((8, 2, 16, 2 * BS), F32),
        ),
        in_specs=[hbm],
        out_specs=(hbm, hbm, hbm),
        scratch_shapes=[
            dma((9,)), dma((9,)), dma((9,)), dma((9,)), dma((8,)), dma((8,)), dma((2,)), dma((2,)),
            dma((15,)), dma((8,)), dma((1,)), dma((1,)), dma((3,)),
        ],
        compiler_params=pltpu.CompilerParams(collective_id=0, has_side_effects=True),
        name="gather_factor",
    )(f_t)
    x = pl.pallas_call(
        product_kernel,
        out_shape=jax.ShapeDtypeStruct((256, LANES), F32),
        in_specs=[smem, smem, hbm, hbm, vmem, vmem, vmem],
        out_specs=vmem,
        scratch_shapes=[
            pltpu.VMEM((2, ROWS, COLS), F32),
            pltpu.VMEM((2, RB, 8, 2, 16, BS), F32),
            pltpu.VMEM((RB // 2, 256, 256), BF16),
            pltpu.VMEM((RB // 2, 256, 256), BF16),
            pltpu.VMEM((256, COLS), F32),
            pltpu.VMEM((256, COLS), BF16),
            pltpu.VMEM((256, COLS), BF16),
            pltpu.VMEM((256, COLS), BF16),
            pltpu.VMEM((256, COLS), BF16),
            pltpu.VMEM((256, COLS), BF16),
            pltpu.VMEM((256, COLS), BF16),
            pltpu.VMEM((256, 256), F32),
            pltpu.SMEM((2, RB + 4), jnp.int32),
            pltpu.SMEM((2, CB + 6), jnp.int32),
            pltpu.SMEM((2, RB + 4), jnp.int32),
            pltpu.SMEM((2, CB + 6), jnp.int32),
            dma((2, RB, CB)),
            dma((2, RB)),
        ],
        compiler_params=pltpu.CompilerParams(vmem_limit_bytes=60 * 1024 * 1024),
        name="products",
    )(row_lists, jnp.swapaxes(pattern, 0, 1), window, fr, fc, q_t, diag_inverse)
    v = lambda *shape: pltpu.VMEM(shape, F32)
    panels, diagonals = pl.pallas_call(
        reduce_kernel,
        out_shape=(
            jax.ShapeDtypeStruct((2, 32, COLS), F32),
            jax.ShapeDtypeStruct((2, 32, BS), F32),
        ),
        in_specs=[vmem],
        out_specs=(vmem, vmem),
        scratch_shapes=[
            v(4, 32, COLS), v(3, 32, COLS), v(32, COLS), v(32, COLS), v(32, COLS), v(16, COLS), v(16, COLS),
            [v(2, 32, SMALL), v(2, 32, COLS)], [v(2, 32, SMALL), v(2, 32, COLS)],
            [v(2, 16, SMALL), v(2, 16, COLS)], [v(2, 16, SMALL), v(2, 16, COLS)],
            [v(2, 2, 32, SMALL), v(2, 2, 32, COLS)],
            [v(32, SMALL), v(32, COLS)], [v(32, SMALL), v(32, COLS)],
            v(32, SMALL), v(32, SMALL), v(8, 16, SMALL), v(32, SMALL),
            dma((6,)), dma((6,)), dma((5, 4)), dma((5, 4)), dma((8,)), dma((8,)), dma((2,)), dma((2,)),
        ],
        compiler_params=pltpu.CompilerParams(collective_id=1, has_side_effects=True),
        name="reduce_sums",
    )(x)
    return jnp.swapaxes(panels, 1, 2), jnp.swapaxes(diagonals, 1, 2)


def solution(mesh):
    in_specs = (P("prow", "pcol"), P("prow", "pcol"), P(), P(None, "prow", "pcol"), P())
    out_specs = (P(None, "pcol", "prow"), P(None, None, "prow"))
    return jax.shard_map(local, mesh=mesh, in_specs=in_specs, out_specs=out_specs, check_vma=False)
```

```python
import jax
import jax.numpy as jnp
from jax import lax
from jax.experimental import pallas as pl
from jax.experimental.pallas import tpu as pltpu
from jax.sharding import PartitionSpec as P

BS = 128
NB = 160
RB = 20
CB = 10
ROWS = RB * BS
COLS = CB * BS
SMALL = 512
LANES = 2 * COLS + SMALL
MESH = pl.DeviceIdType.MESH
F32 = jnp.float32
BF16 = jnp.bfloat16


def remote(src, dst, send, recv, device):
    return pltpu.make_async_remote_copy(
        src_ref=src, dst_ref=dst, send_sem=send, recv_sem=recv, device_id=device, device_id_type=MESH
    )


def coords():
    r = lax.axis_index("prow")
    c = lax.axis_index("pcol")
    return r, c, r // 4, r % 4, c // 8, (c // 2) % 4, c % 2


class PairRing:
    def __init__(self, send, recv, block, half, device, p, y, sent):
        self.s, self.r, self.block, self.half, self.device = send, recv, block, half, device
        self.p, self.y, self.sent = p, y, sent
        self.q = 1 - p
        self.right, self.left, self.far = (y + 1) % 4, (y + 3) % 4, (y + 2) % 4

    def push(self, k, src, dst, device):
        copy = remote(src, dst, self.s.at[k], self.r.at[k], device)
        copy.start()
        self.sent.append(copy)

    def wait(self, k, ref):
        remote(ref, ref, self.s.at[k], self.r.at[k], self.device(self.p, self.right)).wait_recv()

    def start(self, src):
        own = self.block(self.p, self.y)
        self.push(0, src, own, self.device(self.q, self.y))
        self.push(1, src, own, self.device(self.p, self.right))
        self.push(2, src, own, self.device(self.p, self.left))

    def from_left(self, own):
        k, p = (1, self.p) if own else (5, self.q)
        self.wait(k, self.block(p, self.left))
        part = self.half(p, self.left, 0)
        self.push(k + 2, part, part, self.device(self.p, self.right))

    def from_right(self, own):
        k, p = (2, self.p) if own else (6, self.q)
        self.wait(k, self.block(p, self.right))
        part = self.half(p, self.right, 1)
        self.push(k + 2, part, part, self.device(self.p, self.left))

    def from_pair(self):
        other = self.block(self.q, self.y)
        self.wait(0, other)
        self.push(5, other, other, self.device(self.p, self.right))
        self.push(6, other, other, self.device(self.p, self.left))

    def from_far(self, own):
        k, p = (3, self.p) if own else (7, self.q)
        self.wait(k, self.half(p, self.far, 0))
        self.wait(k + 1, self.half(p, self.far, 1))


def split(x):
    hi = x.astype(BF16)
    return hi, (x - hi.astype(F32)).astype(BF16)


def dot3(a, b, nt=False):
    dims = (((1,), (1 if nt else 0,)), ((), ()))
    (ah, al), (bh, bl) = a, b
    one = lambda u, v: lax.dot_general(u, v, dims, preferred_element_type=F32)
    return one(ah, bh) + (one(ah, bl) + one(al, bh))


def kernel(
    rl_ref, pat, w_ref, f_ref, d_ref, panels, diagonals,
    fr, fc, q_ref, w_all, wh, wl, fh, fl, mr, mc, x_ref, x1, ch, cl, c0h, c0l, ph, pw, acc,
    ax, asum, al, ar, ahl, ahr, yl, yr, yhl, yhr, ysum, yx, fin, core, mine, parts, done,
    as_, ar_, bs, br, cs, cr, ts, tr, qs, qr, ks, kr, wsem, local_sem,
    xs, xr, rs, rr, ss, sr, hs, hr,
):
    r, c, xl, y, xh, z, k = coords()
    cc = c // 2
    other = c + 1 - 2 * k
    partner = (r, other)
    diagonal = r == cc
    off_diagonal = jnp.logical_not(diagonal)
    barrier = pltpu.get_barrier_semaphore()

    def greet(device):
        pl.semaphore_signal(barrier, inc=1, device_id=device, device_id_type=MESH)

    @pl.when(off_diagonal)
    def _():
        greet((cc, 2 * r))
        greet((cc, 2 * r + 1))

    for d in range(1, 8):
        greet((r, ((cc + d) % 8) * 2 + k))
        greet(((r + d) % 8, c))
    greet(partner)

    def w_copy(i):
        rows = pl.ds(i * 2 * BS, 2 * BS)
        return pltpu.make_async_copy(w_ref.at[rows], w_all.at[rows], wsem.at[i])

    for i in range(RB // 2):
        w_copy(i).start()

    def mark(dst, first):
        def body(b, carry):
            lanes = pl.ds(pl.multiple_of(b * BS, BS), BS)
            for level in range(2):
                hit = jnp.where(rl_ref[level] == first + b, 1.0, 0.0).astype(F32)
                dst[level, :, lanes] = jnp.broadcast_to(jnp.max(hit, axis=1, keepdims=True), (2, BS))
            return carry

        return body

    lax.fori_loop(0, RB, mark(mr, r * RB), 0)
    lax.fori_loop(0, CB, mark(mc, c * CB), 0)

    @pl.when(off_diagonal)
    def _():
        pl.semaphore_wait(barrier, 17)

    @pl.when(diagonal)
    def _():
        pl.semaphore_wait(barrier, 15)

    sent = []

    def push(src, dst, send, recv, device):
        copy = remote(src, dst, send, recv, device)
        copy.start()
        sent.append(copy)

    def arrived(ref, send, recv):
        remote(ref, ref, send, recv, partner).wait_recv()

    def row_gather(level):
        return PairRing(
            as_.at[level], ar_.at[level],
            lambda p, w: fr.at[level, p * 8 + w * 2 + k],
            lambda p, w, h: fr.at[level, p * 8 + w * 2 + k, pl.ds(8 * h, 8)],
            lambda p, w: (r, p * 8 + w * 2 + k),
            xh, z, sent,
        )

    def column_gather(level):
        return PairRing(
            bs.at[level], br.at[level],
            lambda p, w: fc.at[level, p * 4 + w],
            lambda p, w, h: fc.at[level, p * 4 + w, h],
            lambda p, w: (p * 4 + w, c),
            xl, y, sent,
        )

    ga = [row_gather(0), row_gather(1)]
    gb = [column_gather(0), column_gather(1)]

    def across(level, h):
        return remote(
            f_ref.at[level, :, pl.ds(h * COLS, COLS)], fc.at[level, cc, k], ts.at[level, h], tr.at[level, k],
            (cc, 2 * r + h),
        )

    def across_chip(level):
        return remote(
            f_ref.at[level, :, pl.ds((1 - k) * COLS, COLS)], fc.at[level, cc, k], ts.at[level, 0], tr.at[level, k],
            partner,
        )

    def across_own(level):
        return pltpu.make_async_copy(
            f_ref.at[level, :, pl.ds(k * COLS, COLS)], fc.at[level, r, k], local_sem.at[2 + level]
        )

    @pl.when(off_diagonal)
    def _():
        for level in range(2):
            for h in range(2):
                across(level, h).start()

    @pl.when(diagonal)
    def _():
        for level in range(2):
            across_chip(level).start()
            across_own(level).start()

    last = f_ref.at[1, :, pl.ds(ROWS - 2 * BS, 2 * BS)]
    own_q = q_ref.at[cc, k]

    @pl.when(r == 7)
    def _():
        pltpu.make_async_copy(last, own_q, local_sem.at[0]).start()
        for d in range(7):
            remote(last, own_q, qs.at[d], qr.at[0], (d, c)).start()

    own_copy = [pltpu.make_async_copy(f_ref.at[level], fr.at[level, c], local_sem.at[4 + level]) for level in range(2)]
    for copy in own_copy:
        copy.start()

    def swap(level, chip, src=None):
        block = fr.at[level, chip * 2 + k]
        push(block if src is None else src, block, cs.at[level, chip], cr.at[level, chip], partner)

    right, left, far = (z + 1) % 4, (z + 3) % 4, (z + 2) % 4
    chip = lambda p, w: p * 4 + w

    def row_step(level, step, own):
        side = xh if own else 1 - xh
        if step == "left":
            ga[level].from_left(own)
            swap(level, chip(side, left))
        elif step == "right":
            ga[level].from_right(own)
            swap(level, chip(side, right))
        elif step == "far":
            ga[level].from_far(own)
            swap(level, chip(side, far))
        else:
            ga[level].from_pair()
            swap(level, chip(1 - xh, z))

    def column_start(level):
        @pl.when(off_diagonal)
        def _():
            for h in range(2):
                arrived(fc.at[level, r, h], ts.at[level, h], tr.at[level, h])

        @pl.when(diagonal)
        def _():
            arrived(fc.at[level, r, 1 - k], ts.at[level, 0], tr.at[level, 1 - k])
            across_own(level).wait()

        gb[level].start(fc.at[level, r])

    def split_window(i0, i1):
        for i in range(i0, i1):
            w_copy(i).wait()

        def body(i, carry):
            rows = pl.ds(pl.multiple_of(i * BS, BS), BS)
            row_ok = jnp.where(r * RB + i < NB - 2, 1, 0)
            for j in range(CB):
                lanes = pl.ds(j * BS, BS)
                ok = jnp.where(c * CB + j < NB - 2, 1, 0)
                keep = (pat[j, i] * row_ok * ok).astype(F32)
                wh[rows, lanes], wl[rows, lanes] = split(w_all[rows, lanes] * keep)
            return carry

        lax.fori_loop(2 * i0, 2 * i1, body, 0)

    def split_rows(level):
        def body(b, carry):
            lanes = pl.ds(pl.multiple_of(b * BS, BS), BS)
            for s in range(2):
                rows = pl.ds(s * BS, BS)
                block = fr[level, pl.ds(8 * s, 8), :, lanes].reshape(BS, BS) * mr[level, pl.ds(s, 1), lanes]
                fh[rows, lanes], fl[rows, lanes] = split(block)
            return carry

        lax.fori_loop(0, RB, body, 0)

    def product(n):
        acc[...] = jnp.zeros((256, 256), F32)
        lanes = pl.ds(n * 256, 256)

        def body(i, carry):
            depth = pl.ds(pl.multiple_of(i * 512, 512), 512)
            acc[...] += dot3((fh[:, depth], fl[:, depth]), (wh[depth, lanes], wl[depth, lanes]))
            return carry

        lax.fori_loop(0, RB // 4, body, 0)

    def first_level(n):
        product(n)
        lanes = pl.ds(n * 256, 256)
        for s in range(2):
            rows = pl.ds(s * BS, BS)
            x_ref[rows, lanes] = -(acc[rows, :] * mc[0, pl.ds(s, 1), lanes])

    def second_level(n):
        product(n)
        x1[:, pl.ds(n * 256, 256)] = acc[...]

    ga[0].start(f_ref.at[0])
    swap(0, cc, f_ref.at[0])
    split_window(0, 4)

    @pl.when(r == 7)
    def _():
        pltpu.make_async_copy(last, own_q, local_sem.at[0]).wait()

    @pl.when(r != 7)
    def _():
        arrived(own_q, qs.at[0], qr.at[0])

    for d in range(1, 8):
        push(own_q, own_q, qs.at[7 + d], qr.at[d], (r, ((cc + d) % 8) * 2 + k))
    row_step(0, "left", True)
    row_step(0, "right", True)
    ga[1].start(f_ref.at[1])
    swap(1, cc, f_ref.at[1])
    column_start(0)
    column_start(1)
    row_step(0, "pair", True)
    split_window(4, 7)
    gb[0].from_left(True)
    gb[0].from_right(True)
    row_step(0, "far", True)
    row_step(1, "left", True)
    row_step(1, "right", True)
    gb[0].from_pair()
    row_step(1, "pair", True)
    gb[1].from_left(True)
    gb[1].from_right(True)
    row_step(0, "left", False)
    row_step(0, "right", False)
    split_window(7, 10)
    gb[1].from_pair()
    gb[0].from_far(True)
    gb[0].from_left(False)
    gb[0].from_right(False)
    row_step(1, "far", True)
    row_step(0, "far", False)
    for d in range(1, 8):
        arrived(q_ref.at[(cc + 8 - d) % 8, k], qs.at[0], qr.at[d])
    half = q_ref.at[:, k]
    push(half, half, ks.at[0], kr.at[0], partner)
    for m in range(8):
        arrived(fr.at[0, m * 2 + 1 - k], cs.at[0, m], cr.at[0, m])
    own_copy[0].wait()

    split_rows(0)
    first_level(0)
    row_step(1, "left", False)
    row_step(1, "right", False)
    first_level(1)
    gb[1].from_far(True)
    gb[1].from_left(False)
    gb[1].from_right(False)
    first_level(2)
    gb[0].from_far(False)
    row_step(1, "far", False)
    first_level(3)
    first_level(4)

    px = (4 * (1 - xl) + y, c)
    yright, yleft, yfar = (y + 1) % 4, (y + 3) % 4, (y + 2) % 4
    dr, dl = (4 * xl + yright, c), (4 * xl + yleft, c)

    def rows_of(p, w, h=None):
        if h is None:
            return pl.ds(pl.multiple_of((4 * p + w) * 32, 32), 32)
        return pl.ds(pl.multiple_of((4 * p + w) * 32 + 16 * h, 16), 16)

    lane_a = pl.ds(0, COLS)
    streams = ((2 * COLS, SMALL), (COLS, COLS))

    def ring_first(t, p, v):
        start, width = streams[t]
        lanes = pl.ds(start, width)
        e = 2 * t + v
        push(x_ref.at[rows_of(p, yfar, 0), lanes], yhl[t].at[v], rs.at[e, 0], rr.at[e, 0], dr)
        push(x_ref.at[rows_of(p, yfar, 1), lanes], yhr[t].at[v], rs.at[e, 1], rr.at[e, 1], dl)

    def ring_second(t, p, v):
        start, width = streams[t]
        lanes = pl.ds(start, width)
        e = 2 * t + v
        arrived(yhl[t].at[v], rs.at[e, 0], rr.at[e, 0])
        ysum[t][v, 0, pl.ds(0, 16), :] = x_ref[rows_of(p, yright, 0), lanes] + yhl[t][v]
        ysum[t][v, 0, pl.ds(16, 16), :] = x_ref[rows_of(p, yright, 1), lanes]
        push(ysum[t].at[v, 0], yl[t].at[v], rs.at[e, 2], rr.at[e, 2], dr)
        arrived(yhr[t].at[v], rs.at[e, 1], rr.at[e, 1])
        ysum[t][v, 1, pl.ds(0, 16), :] = x_ref[rows_of(p, yleft, 0), lanes]
        ysum[t][v, 1, pl.ds(16, 16), :] = x_ref[rows_of(p, yleft, 1), lanes] + yhr[t][v]
        push(ysum[t].at[v, 1], yr[t].at[v], rs.at[e, 3], rr.at[e, 3], dl)

    def ring_third(t, p, v):
        start, width = streams[t]
        e = 2 * t + v
        arrived(yl[t].at[v], rs.at[e, 2], rr.at[e, 2])
        arrived(yr[t].at[v], rs.at[e, 3], rr.at[e, 3])
        return x_ref[rows_of(p, y), pl.ds(start, width)] + (yl[t][v] + yr[t][v])

    q = 1 - xl
    for w, d in ((0, yfar), (1, yright), (2, yleft), (3, y)):
        push(x_ref.at[rows_of(q, d), lane_a], ax.at[w], xs.at[w], xr.at[w], px)

    for m in range(8):
        arrived(fr.at[1, m * 2 + 1 - k], cs.at[1, m], cr.at[1, m])
    own_copy[1].wait()
    split_rows(1)
    second_level(0)
    arrived(ax.at[0], xs.at[0], xr.at[0])
    asum[0] = x_ref[rows_of(xl, yfar), lane_a] + ax[0]
    push(asum.at[0, pl.ds(0, 16)], ahl, rs.at[4, 0], rr.at[4, 0], dr)
    push(asum.at[0, pl.ds(16, 16)], ahr, rs.at[4, 1], rr.at[4, 1], dl)
    second_level(1)
    gb[1].from_far(False)
    second_level(2)
    arrived(ax.at[1], xs.at[1], xr.at[1])
    asum[1] = x_ref[rows_of(xl, yright), lane_a] + ax[1]
    arrived(ahl, rs.at[4, 0], rr.at[4, 0])
    asum[1, pl.ds(0, 16)] = asum[1, pl.ds(0, 16)] + ahl[...]
    push(asum.at[1], al, rs.at[4, 2], rr.at[4, 2], dr)
    second_level(3)
    arrived(ax.at[2], xs.at[2], xr.at[2])
    asum[2] = x_ref[rows_of(xl, yleft), lane_a] + ax[2]
    arrived(ahr, rs.at[4, 1], rr.at[4, 1])
    asum[2, pl.ds(16, 16)] = asum[2, pl.ds(16, 16)] + ahr[...]
    push(asum.at[2], ar, rs.at[4, 3], rr.at[4, 3], dl)
    second_level(4)

    for s in range(2):
        rows = pl.ds(s * BS, BS)

        def body(j, carry):
            lanes = pl.ds(pl.multiple_of(j * BS, BS), BS)
            block = fc[1, pl.ds(4 * s, 4), :, :, lanes].reshape(BS, BS) * mc[1, pl.ds(s, 1), lanes]
            ch[rows, lanes], cl[rows, lanes] = split(block)
            block = fc[0, pl.ds(4 * s, 4), :, :, lanes].reshape(BS, BS)
            c0h[rows, lanes], c0l[rows, lanes] = split(block)
            return carry

        lax.fori_loop(0, CB, body, 0)
    half = q_ref.at[:, 1 - k]
    arrived(half, ks.at[0], kr.at[0])
    qv = split(q_ref[...].reshape(256, 256))
    ph[...], pw[...] = split(x_ref[:, lane_a])
    pair = lambda h, l, rows: (h[rows, :], l[rows, :])
    whole = pl.ds(0, 256)
    a_t = dot3(pair(ch, cl, whole), pair(ph, pw, whole), nt=True)
    chosen = jnp.where(jnp.logical_and(r == 0, c == 0), 1.0, 0.0).astype(F32)
    s_t = []
    for s in range(2):
        rows = pl.ds(s * BS, BS)
        s_t.append(chosen * d_ref[0, :, rows] - dot3(pair(ph, pw, rows), pair(c0h, c0l, rows), nt=True))
    slot = a_t + jnp.concatenate(
        [dot3((qv[0][:, s * BS:(s + 1) * BS], qv[1][:, s * BS:(s + 1) * BS]), split(s_t[s])) for s in range(2)], axis=1
    )
    a_s, slot_s = split(a_t), split(slot)
    base = 2 * COLS
    for s in range(2):
        rows = pl.ds(s * BS, BS)
        cut = lambda v: (v[0][s * BS:(s + 1) * BS], v[1][s * BS:(s + 1) * BS])
        second = (
            chosen * d_ref[1, :, rows]
            + dot3(split(x1[rows, :]), pair(ch, cl, rows), nt=True)
            + dot3(cut(qv), cut(a_s), nt=True)
            + dot3(cut(slot_s), cut(qv), nt=True)
        )
        x_ref[rows, pl.ds(base, BS)] = s_t[s]
        x_ref[rows, pl.ds(base + BS, BS)] = second
        x_ref[rows, pl.ds(base + 2 * BS, 2 * BS)] = -slot[s * BS:(s + 1) * BS]
    ring_first(0, q, 0)
    ring_first(0, xl, 1)

    def second_sum(n, carry):
        lanes = pl.ds(pl.multiple_of(n * 256, 256), 256)
        full = x1[:, lanes] + dot3(qv, (ph[:, lanes], pw[:, lanes]))
        out = pl.ds(pl.multiple_of(COLS + n * 256, 256), 256)
        for s in range(2):
            x_ref[pl.ds(s * BS, BS), out] = -(full[s * BS:(s + 1) * BS] * mc[1, pl.ds(s, 1), lanes])
        return carry

    lax.fori_loop(0, CB // 2, second_sum, 0)
    ring_first(1, q, 0)
    ring_second(0, q, 0)
    ring_second(0, xl, 1)
    ring_first(1, xl, 1)
    ring_second(1, q, 0)

    fin[0][...] = ring_third(0, q, 0)
    push(fin[0], yx[0], xs.at[4], xr.at[4], px)
    ring_second(1, xl, 1)
    small = ring_third(0, xl, 1)
    arrived(yx[0], xs.at[4], xr.at[4])
    mine[...] = small + yx[0][...]
    push(mine, core, hs.at[0], hr.at[0], partner)
    arrived(core, hs.at[0], hr.at[0])
    own_half = pl.ds(pl.multiple_of(16 * k, 16), 16)
    parts[cc] = mine[own_half, :] + core[own_half, :]
    for d in range(1, 8):
        push(parts.at[cc], parts.at[cc], ss.at[d], sr.at[d], (r, ((cc + d) % 8) * 2 + k))

    fin[1][...] = ring_third(1, q, 0)
    push(fin[1], yx[1], xs.at[5], xr.at[5], px)

    arrived(ax.at[3], xs.at[3], xr.at[3])
    first = x_ref[rows_of(xl, y), lane_a] + ax[3]
    arrived(al, rs.at[4, 2], rr.at[4, 2])
    arrived(ar, rs.at[4, 3], rr.at[4, 3])
    panels[0] = first + (al[...] + ar[...])

    for d in range(1, 8):
        arrived(parts.at[(cc + 8 - d) % 8], ss.at[d], sr.at[d])
    total = parts[0]
    for d in range(1, 8):
        total = total + parts[d]
    done[own_half, :] = total
    push(done.at[own_half], done.at[own_half], hs.at[1], hr.at[1], partner)

    second = ring_third(1, xl, 1)
    arrived(yx[1], xs.at[5], xr.at[5])
    panels[1] = second + yx[1][...]
    other_half = pl.ds(pl.multiple_of(16 * (1 - k), 16), 16)
    arrived(done.at[other_half], hs.at[1], hr.at[1])
    diagonals[0] = done[:, pl.ds(0, BS)]
    diagonals[1] = done[:, pl.ds(BS, BS)]
    at_end = jnp.where(c == 15, 1.0, 0.0).astype(F32)
    tail = pl.ds(COLS - 2 * BS, 2 * BS)
    panels[1, :, tail] = panels[1, :, tail] + at_end * done[:, pl.ds(2 * BS, 2 * BS)]
    for copy in sent:
        copy.wait_send()

    @pl.when(r == 7)
    def _():
        for d in range(7):
            remote(last, own_q, qs.at[d], qr.at[0], (d, c)).wait_send()

    @pl.when(off_diagonal)
    def _():
        for level in range(2):
            for h in range(2):
                across(level, h).wait_send()

    @pl.when(diagonal)
    def _():
        for level in range(2):
            across_chip(level).wait_send()


def local(window, pattern, row_lists, factor, diag_inverse):
    dma = pltpu.SemaphoreType.DMA
    hbm = pl.BlockSpec(memory_space=pl.ANY)
    vmem = pl.BlockSpec(memory_space=pltpu.VMEM)
    smem = pl.BlockSpec(memory_space=pltpu.SMEM)
    v = lambda *shape: pltpu.VMEM(shape, F32)
    h = lambda *shape: pltpu.VMEM(shape, BF16)
    both = lambda *shape: [v(*shape, SMALL), v(*shape, COLS)]
    panels, diagonals = pl.pallas_call(
        kernel,
        out_shape=(
            jax.ShapeDtypeStruct((2, 32, COLS), F32),
            jax.ShapeDtypeStruct((2, 32, BS), F32),
        ),
        in_specs=[vmem, smem, hbm, hbm, vmem],
        out_specs=(vmem, vmem),
        scratch_shapes=[
            v(2, 16, 16, ROWS), v(2, 8, 2, 16, COLS), v(8, 2, 16, 2 * BS), v(ROWS, COLS), h(ROWS, COLS), h(ROWS, COLS),
            h(256, ROWS), h(256, ROWS), v(2, 2, ROWS), v(2, 2, COLS), v(256, LANES), v(256, COLS),
            h(256, COLS), h(256, COLS), h(256, COLS), h(256, COLS), h(256, COLS), h(256, COLS), v(256, 256),
            v(4, 32, COLS), v(3, 32, COLS), v(32, COLS), v(32, COLS), v(16, COLS), v(16, COLS),
            both(2, 32), both(2, 32), both(2, 16), both(2, 16), both(2, 2, 32), both(32), both(32),
            v(32, SMALL), v(32, SMALL), v(8, 16, SMALL), v(32, SMALL),
            dma((2, 9)), dma((2, 9)), dma((2, 9)), dma((2, 9)), dma((2, 8)), dma((2, 8)), dma((2, 2)), dma((2, 2)),
            dma((15,)), dma((8,)), dma((1,)), dma((1,)), dma((RB // 2,)), dma((6,)),
            dma((6,)), dma((6,)), dma((5, 4)), dma((5, 4)), dma((8,)), dma((8,)), dma((2,)), dma((2,)),
        ],
        compiler_params=pltpu.CompilerParams(
            collective_id=0, has_side_effects=True, vmem_limit_bytes=63 * 1024 * 1024
        ),
        name="selected_inversion",
    )(row_lists, jnp.swapaxes(pattern, 0, 1), window, jnp.swapaxes(factor, 1, 2), diag_inverse)
    return jnp.swapaxes(panels, 1, 2), jnp.swapaxes(diagonals, 1, 2)


def solution(mesh):
    in_specs = (P("prow", "pcol"), P("prow", "pcol"), P(), P(None, "prow", "pcol"), P())
    out_specs = (P(None, "pcol", "prow"), P(None, None, "prow"))
    return jax.shard_map(local, mesh=mesh, in_specs=in_specs, out_specs=out_specs, check_vma=False)
```

```python
import jax
import jax.numpy as jnp
from jax import lax
from jax.experimental import pallas as pl
from jax.experimental.pallas import tpu as pltpu
from jax.sharding import PartitionSpec as P

BS = 128
NB = 160
RB = 20
CB = 10
ROWS = RB * BS
COLS = CB * BS
SMALL = 512
CROSS = 6 * BS
MESH = pl.DeviceIdType.MESH
F32 = jnp.float32
BF16 = jnp.bfloat16


def remote(src, dst, send, recv, device):
    return pltpu.make_async_remote_copy(
        src_ref=src, dst_ref=dst, send_sem=send, recv_sem=recv, device_id=device, device_id_type=MESH
    )


def coords():
    r = lax.axis_index("prow")
    c = lax.axis_index("pcol")
    return r, c, r // 4, r % 4, c // 8, (c // 2) % 4, c % 2


class PairRing:
    def __init__(self, send, recv, block, half, device, p, y, sent):
        self.s, self.r, self.block, self.half, self.device = send, recv, block, half, device
        self.p, self.y, self.sent = p, y, sent
        self.q = 1 - p
        self.right, self.left, self.far = (y + 1) % 4, (y + 3) % 4, (y + 2) % 4

    def push(self, k, src, dst, device):
        copy = remote(src, dst, self.s.at[k], self.r.at[k], device)
        copy.start()
        self.sent.append(copy)

    def wait(self, k, ref):
        remote(ref, ref, self.s.at[k], self.r.at[k], self.device(self.p, self.right)).wait_recv()

    def start_pair(self, src):
        self.push(0, src, self.block(self.p, self.y), self.device(self.q, self.y))

    def start_ring(self, src):
        own = self.block(self.p, self.y)
        self.push(1, src, own, self.device(self.p, self.right))
        self.push(2, src, own, self.device(self.p, self.left))

    def from_left(self, own):
        k, p = (1, self.p) if own else (5, self.q)
        self.wait(k, self.block(p, self.left))
        part = self.half(p, self.left, 0)
        self.push(k + 2, part, part, self.device(self.p, self.right))

    def from_right(self, own):
        k, p = (2, self.p) if own else (6, self.q)
        self.wait(k, self.block(p, self.right))
        part = self.half(p, self.right, 1)
        self.push(k + 2, part, part, self.device(self.p, self.left))

    def from_pair(self):
        other = self.block(self.q, self.y)
        self.wait(0, other)
        self.push(5, other, other, self.device(self.p, self.right))
        self.push(6, other, other, self.device(self.p, self.left))

    def from_far(self, own):
        k, p = (3, self.p) if own else (7, self.q)
        self.wait(k, self.half(p, self.far, 0))
        self.wait(k + 1, self.half(p, self.far, 1))


def split(x):
    hi = x.astype(BF16)
    return hi, (x - hi.astype(F32)).astype(BF16)


def dot3(a, b, nt=False):
    dims = (((1,), (1 if nt else 0,)), ((), ()))
    (ah, al), (bh, bl) = a, b
    one = lambda u, v: lax.dot_general(u, v, dims, preferred_element_type=F32)
    return one(ah, bh) + (one(ah, bl) + one(al, bh))


def kernel(
    rl_ref, pat, w_ref, f_ref, d_ref, out,
    fr, fc, q_ref, w_all, wh, wl, fh, fl, mr, mc, x_ref, x1, ch, cl, c0h, c0l, ph, pw, acc,
    ax, asum, al, ar, ahl, ahr, yin, yx, fin, bx, bsum, byin, small, core, mine, rows_in, parts, done,
    as_, ar_, bs, br, cs, cr, ts, tr, qs, qr, ks, kr, wsem, local_sem,
    xs, xr, rs, rr, ss, sr, hs, hr, gs, gr, es, er, us, ur,
):
    r, c, xl, y, xh, z, k = coords()
    cc = c // 2
    other = c + 1 - 2 * k
    partner = (r, other)
    to_row = xh * 4 + (y + z) % 4
    got = xl * 4 + (y + 4 - z) % 4
    diagonal = jnp.logical_and(xl == xh, jnp.logical_and(y == 0, z == 0))
    off_diagonal = jnp.logical_not(diagonal)
    barrier = pltpu.get_barrier_semaphore()

    def greet(device):
        pl.semaphore_signal(barrier, inc=1, device_id=device, device_id_type=MESH)

    @pl.when(off_diagonal)
    def _():
        for h in range(2):
            greet((to_row, 2 * r + h))
            greet((cc, 2 * got + h))

    for d in range(1, 8):
        greet((r, ((cc + d) % 8) * 2 + k))
        greet(((r + d) % 8, c))
    greet(partner)

    def w_copy(i):
        rows = pl.ds(i * 2 * BS, 2 * BS)
        return pltpu.make_async_copy(w_ref.at[rows], w_all.at[rows], wsem.at[i])

    for i in range(RB // 2):
        w_copy(i).start()

    def mark(dst, first):
        def body(b, carry):
            lanes = pl.ds(pl.multiple_of(b * BS, BS), BS)
            for level in range(2):
                hit = jnp.where(rl_ref[level] == first + b, 1.0, 0.0).astype(F32)
                dst[level, :, lanes] = jnp.broadcast_to(jnp.max(hit, axis=1, keepdims=True), (2, BS))
            return carry

        return body


    @pl.when(off_diagonal)
    def _():
        pl.semaphore_wait(barrier, 19)

    @pl.when(diagonal)
    def _():
        pl.semaphore_wait(barrier, 15)

    sent = []

    def push(src, dst, send, recv, device):
        copy = remote(src, dst, send, recv, device)
        copy.start()
        sent.append(copy)

    def arrived(ref, send, recv):
        remote(ref, ref, send, recv, partner).wait_recv()

    def row_gather(level):
        return PairRing(
            as_.at[level], ar_.at[level],
            lambda p, w: fr.at[level, p * 8 + w * 2 + k],
            lambda p, w, h: fr.at[level, p * 8 + w * 2 + k, pl.ds(8 * h, 8)],
            lambda p, w: (r, p * 8 + w * 2 + k),
            xh, z, sent,
        )

    def column_gather(level):
        return PairRing(
            bs.at[level], br.at[level],
            lambda p, w: fc.at[level, p * 4 + (w + 4 - z) % 4],
            lambda p, w, h: fc.at[level, p * 4 + (w + 4 - z) % 4, h],
            lambda p, w: (p * 4 + w, c),
            xl, y, sent,
        )

    ga = [row_gather(0), row_gather(1)]
    gb = [column_gather(0), column_gather(1)]

    def across(level, h):
        return remote(
            f_ref.at[level, :, pl.ds(h * COLS, COLS)], fc.at[level, cc, k], ts.at[level, h], tr.at[level, k],
            (to_row, 2 * r + h),
        )

    def across_chip(level):
        return remote(
            f_ref.at[level, :, pl.ds((1 - k) * COLS, COLS)], fc.at[level, cc, k], ts.at[level, 0], tr.at[level, k],
            partner,
        )

    def across_own(level):
        return pltpu.make_async_copy(
            f_ref.at[level, :, pl.ds(k * COLS, COLS)], fc.at[level, cc, k], local_sem.at[2 + level]
        )

    @pl.when(off_diagonal)
    def _():
        for level in range(2):
            for h in range(2):
                across(level, h).start()

    @pl.when(diagonal)
    def _():
        for level in range(2):
            across_chip(level).start()
            across_own(level).start()

    last = f_ref.at[1, :, pl.ds(ROWS - 2 * BS, 2 * BS)]
    own_q = q_ref.at[cc, k]

    @pl.when(r == 7)
    def _():
        pltpu.make_async_copy(last, own_q, local_sem.at[0]).start()
        for d in range(7):
            remote(last, own_q, qs.at[d], qr.at[0], (d, c)).start()

    own_copy = [pltpu.make_async_copy(f_ref.at[level], fr.at[level, c], local_sem.at[4 + level]) for level in range(2)]
    for copy in own_copy:
        copy.start()

    def swap(level, chip, src=None):
        block = fr.at[level, chip * 2 + k]
        push(block if src is None else src, block, cs.at[level, chip], cr.at[level, chip], partner)

    right, left, far = (z + 1) % 4, (z + 3) % 4, (z + 2) % 4
    chip = lambda p, w: p * 4 + w

    def row_step(level, step, own):
        side = xh if own else 1 - xh
        if step == "left":
            ga[level].from_left(own)
            swap(level, chip(side, left))
        elif step == "right":
            ga[level].from_right(own)
            swap(level, chip(side, right))
        elif step == "far":
            ga[level].from_far(own)
            swap(level, chip(side, far))
        else:
            ga[level].from_pair()
            swap(level, chip(1 - xh, z))

    def column_start(level):
        @pl.when(off_diagonal)
        def _():
            for h in range(2):
                arrived(fc.at[level, got, h], ts.at[level, h], tr.at[level, h])

        @pl.when(diagonal)
        def _():
            arrived(fc.at[level, got, 1 - k], ts.at[level, 0], tr.at[level, 1 - k])
            across_own(level).wait()

        gb[level].start_pair(fc.at[level, got])
        gb[level].start_ring(fc.at[level, got])

    def split_window(i0, i1):
        for i in range(i0, i1):
            w_copy(i).wait()

        def body(i, carry):
            rows = pl.ds(pl.multiple_of(i * BS, BS), BS)
            row_ok = jnp.where(r * RB + i < NB - 2, 1, 0)
            for j in range(CB):
                lanes = pl.ds(j * BS, BS)
                ok = jnp.where(c * CB + j < NB - 2, 1, 0)
                keep = (pat[j, i] * row_ok * ok).astype(F32)
                wh[rows, lanes], wl[rows, lanes] = split(w_all[rows, lanes] * keep)
            return carry

        lax.fori_loop(2 * i0, 2 * i1, body, 0)

    def split_rows(level):
        def body(b, carry):
            lanes = pl.ds(pl.multiple_of(b * BS, BS), BS)
            for s in range(2):
                rows = pl.ds(s * BS, BS)
                block = fr[level, pl.ds(8 * s, 8), :, lanes].reshape(BS, BS) * mr[level, pl.ds(s, 1), lanes]
                fh[rows, lanes], fl[rows, lanes] = split(block)
            return carry

        lax.fori_loop(0, RB, body, 0)

    def product(n):
        acc[...] = jnp.zeros((256, 256), F32)
        lanes = pl.ds(n * 256, 256)

        def body(i, carry):
            depth = pl.ds(pl.multiple_of(i * 512, 512), 512)
            acc[...] += dot3((fh[:, depth], fl[:, depth]), (wh[depth, lanes], wl[depth, lanes]))
            return carry

        lax.fori_loop(0, RB // 4, body, 0)

    def first_level(n):
        product(n)
        lanes = pl.ds(n * 256, 256)
        for s in range(2):
            rows = pl.ds(s * BS, BS)
            x_ref[rows, lanes] = -(acc[rows, :] * mc[0, pl.ds(s, 1), lanes])

    def second_level(n):
        product(n)
        x1[:, pl.ds(n * 256, 256)] = acc[...]

    def q_spread():
        @pl.when(r == 7)
        def _():
            pltpu.make_async_copy(last, own_q, local_sem.at[0]).wait()

        @pl.when(r != 7)
        def _():
            arrived(own_q, qs.at[0], qr.at[0])

        for d in range(1, 8):
            push(own_q, own_q, qs.at[7 + d], qr.at[d], (r, ((cc + d) % 8) * 2 + k))

    def q_swap():
        for d in range(1, 8):
            arrived(q_ref.at[(cc + 8 - d) % 8, k], qs.at[0], qr.at[d])
        half = q_ref.at[:, k]
        push(half, half, ks.at[0], kr.at[0], partner)

    def swapped(level):
        for m in range(8):
            arrived(fr.at[level, m * 2 + 1 - k], cs.at[level, m], cr.at[level, m])
        own_copy[level].wait()

    ga[0].start_pair(f_ref.at[0])
    ga[0].start_ring(f_ref.at[0])
    ga[1].start_pair(f_ref.at[1])
    for level in range(2):
        swap(level, cc, f_ref.at[level])
    lax.fori_loop(0, RB, mark(mr, r * RB), 0)
    row_step(0, "left", True)
    row_step(0, "right", True)
    q_spread()
    row_step(0, "pair", True)
    split_window(0, 4)
    column_start(0)
    column_start(1)
    row_step(0, "far", True)
    lax.fori_loop(0, CB, mark(mc, c * CB), 0)
    row_step(0, "left", False)
    row_step(0, "right", False)
    ga[1].start_ring(f_ref.at[1])
    row_step(1, "pair", True)
    split_window(4, 7)
    q_swap()
    gb[0].from_left(True)
    gb[0].from_right(True)
    row_step(0, "far", False)
    split_window(7, 10)
    gb[0].from_pair()
    gb[1].from_pair()
    swapped(0)

    split_rows(0)
    first_level(0)
    gb[1].from_left(True)
    gb[1].from_right(True)
    row_step(1, "left", True)
    row_step(1, "right", True)
    first_level(1)
    first_level(2)
    gb[0].from_far(True)
    row_step(1, "far", True)
    row_step(1, "left", False)
    row_step(1, "right", False)
    first_level(3)
    first_level(4)

    px = (4 * (1 - xl) + y, c)
    yright, yleft, yfar = (y + 1) % 4, (y + 3) % 4, (y + 2) % 4
    dr, dl = (4 * xl + yright, c), (4 * xl + yleft, c)

    def rows_of(p, w, h=None):
        if h is None:
            return pl.ds(pl.multiple_of((4 * p + w) * 32, 32), 32)
        return pl.ds(pl.multiple_of((4 * p + w) * 32 + 16 * h, 16), 16)

    lane_a = pl.ds(0, COLS)
    lane_c = pl.ds(COLS + CROSS, COLS - CROSS)
    lane_b = pl.ds(COLS, CROSS)
    dfar = (4 * xl + yfar, c)
    along = ((0, yright, dr), (1, yleft, dl), (2, yfar, dfar))

    def spread(p, v):
        for i, w, device in along:
            push(x_ref.at[rows_of(p, w), lane_c], yin.at[v, i], rs.at[v, i], rr.at[v, i], device)

    def collect(p, v):
        for i in range(3):
            arrived(yin.at[v, i], rs.at[v, i], rr.at[v, i])
        return (x_ref[rows_of(p, y), lane_c] + yin[v, 0]) + (yin[v, 1] + yin[v, 2])

    q = 1 - xl
    for w, d in ((0, yfar), (1, yright), (2, yleft), (3, y)):
        push(x_ref.at[rows_of(q, d), lane_a], ax.at[w], xs.at[w], xr.at[w], px)

    gb[0].from_left(False)
    gb[0].from_right(False)
    gb[1].from_far(True)
    gb[1].from_left(False)
    gb[1].from_right(False)
    row_step(1, "far", False)
    swapped(1)
    split_rows(1)
    second_level(0)
    arrived(ax.at[0], xs.at[0], xr.at[0])
    asum[0] = x_ref[rows_of(xl, yfar), lane_a] + ax[0]
    push(asum.at[0, pl.ds(0, 16)], ahl, rs.at[4, 0], rr.at[4, 0], dr)
    push(asum.at[0, pl.ds(16, 16)], ahr, rs.at[4, 1], rr.at[4, 1], dl)
    second_level(1)
    gb[0].from_far(False)
    second_level(2)
    arrived(ax.at[1], xs.at[1], xr.at[1])
    asum[1] = x_ref[rows_of(xl, yright), lane_a] + ax[1]
    arrived(ahl, rs.at[4, 0], rr.at[4, 0])
    asum[1, pl.ds(0, 16)] = asum[1, pl.ds(0, 16)] + ahl[...]
    push(asum.at[1], al, rs.at[4, 2], rr.at[4, 2], dr)
    second_level(3)
    arrived(ax.at[2], xs.at[2], xr.at[2])
    asum[2] = x_ref[rows_of(xl, yleft), lane_a] + ax[2]
    arrived(ahr, rs.at[4, 1], rr.at[4, 1])
    asum[2, pl.ds(16, 16)] = asum[2, pl.ds(16, 16)] + ahr[...]
    push(asum.at[2], ar, rs.at[4, 3], rr.at[4, 3], dl)
    second_level(4)

    half = q_ref.at[:, 1 - k]
    arrived(half, ks.at[0], kr.at[0])
    qv = split(q_ref[...].reshape(256, 256))
    ph[...], pw[...] = split(x_ref[:, lane_a])
    def second_sum(n, carry):
        lanes = pl.ds(pl.multiple_of(n * 256, 256), 256)
        full = x1[:, lanes] + dot3(qv, (ph[:, lanes], pw[:, lanes]))
        out = pl.ds(pl.multiple_of(COLS + n * 256, 256), 256)
        for s in range(2):
            x_ref[pl.ds(s * BS, BS), out] = -(full[s * BS:(s + 1) * BS] * mc[1, pl.ds(s, 1), lanes])
        return carry

    lax.fori_loop(0, CB // 2, second_sum, 0)
    spread(q, 0)
    for w, d in ((0, yfar), (1, yright), (2, yleft), (3, y)):
        push(x_ref.at[rows_of(q, d), lane_b], bx.at[w], gs.at[w], gr.at[w], px)
    spread(xl, 1)

    gb[1].from_far(False)
    for s in range(2):
        rows = pl.ds(s * BS, BS)

        def body(j, carry):
            lanes = pl.ds(pl.multiple_of(j * BS, BS), BS)
            block = fc[1, pl.ds(4 * s, 4), :, :, lanes].reshape(BS, BS) * mc[1, pl.ds(s, 1), lanes]
            ch[rows, lanes], cl[rows, lanes] = split(block)
            block = fc[0, pl.ds(4 * s, 4), :, :, lanes].reshape(BS, BS)
            c0h[rows, lanes], c0l[rows, lanes] = split(block)
            return carry

        lax.fori_loop(0, CB, body, 0)
    pair = lambda h, l, rows: (h[rows, :], l[rows, :])
    whole = pl.ds(0, 256)
    a_t = dot3(pair(ch, cl, whole), pair(ph, pw, whole), nt=True)
    chosen = jnp.where(jnp.logical_and(r == 0, c == 0), 1.0, 0.0).astype(F32)
    s_t = []
    for s in range(2):
        rows = pl.ds(s * BS, BS)
        s_t.append(chosen * d_ref[0, :, rows] - dot3(pair(ph, pw, rows), pair(c0h, c0l, rows), nt=True))
    slot = a_t + jnp.concatenate(
        [dot3((qv[0][:, s * BS:(s + 1) * BS], qv[1][:, s * BS:(s + 1) * BS]), split(s_t[s])) for s in range(2)], axis=1
    )
    a_s, slot_s = split(a_t), split(slot)
    for s in range(2):
        rows = pl.ds(s * BS, BS)
        cut = lambda v: (v[0][s * BS:(s + 1) * BS], v[1][s * BS:(s + 1) * BS])
        second = (
            chosen * d_ref[1, :, rows]
            + dot3(split(x1[rows, :]), pair(ch, cl, rows), nt=True)
            + dot3(cut(qv), cut(a_s), nt=True)
            + dot3(cut(slot_s), cut(qv), nt=True)
        )
        for lanes, value in (
            (pl.ds(0, BS), s_t[s]), (pl.ds(BS, BS), second), (pl.ds(2 * BS, 2 * BS), -slot[s * BS:(s + 1) * BS])
        ):
            small[pl.ds(4 * s, 4), :, :, lanes] = value.reshape(4, 2, 16, value.shape[1])
    theirs = small.at[:, 1 - k]
    push(theirs, core, hs.at[0], hr.at[0], partner)

    def crossed(w, i, d, device):
        arrived(bx.at[w], gs.at[w], gr.at[w])
        bsum[i] = x_ref[rows_of(xl, d), lane_b] + bx[w]
        push(bsum.at[i], byin.at[i], es.at[i], er.at[i], device)

    arrived(core, hs.at[0], hr.at[0])
    mine[...] = small[:, k] + core[...]
    for d in range(1, 8):
        to = (r + d) % 8
        push(mine.at[to], rows_in.at[d - 1], us.at[d], ur.at[d], (to, c))
    crossed(0, 2, yfar, dfar)
    crossed(1, 0, yright, dr)
    crossed(2, 1, yleft, dl)
    total = mine[r]
    for d in range(1, 8):
        arrived(rows_in.at[d - 1], us.at[d], ur.at[d])
        total = total + rows_in[d - 1]
    parts[cc] = total
    for d in range(1, 8):
        push(parts.at[cc], parts.at[cc], ss.at[d], sr.at[d], (r, ((cc + d) % 8) * 2 + k))
    fin[...] = collect(q, 0)
    push(fin, yx, xs.at[5], xr.at[5], px)

    arrived(ax.at[3], xs.at[3], xr.at[3])
    first = x_ref[rows_of(xl, y), lane_a] + ax[3]
    arrived(al, rs.at[4, 2], rr.at[4, 2])
    arrived(ar, rs.at[4, 3], rr.at[4, 3])
    out[0, :, lane_a] = first + (al[...] + ar[...])

    own_half = pl.ds(pl.multiple_of(16 * k, 16), 16)
    for d in range(1, 8):
        arrived(parts.at[(cc + 8 - d) % 8], ss.at[d], sr.at[d])
    total = parts[0]
    for d in range(1, 8):
        total = total + parts[d]
    done[own_half, :] = total
    push(done.at[own_half], done.at[own_half], hs.at[1], hr.at[1], partner)

    lane_d = pl.ds(CROSS, COLS - CROSS)
    lane_e = pl.ds(COLS, BS)
    out[1, :, lane_d] = collect(xl, 1)
    arrived(bx.at[3], gs.at[3], gr.at[3])
    second = x_ref[rows_of(xl, y), lane_b] + bx[3]
    arrived(yx, xs.at[5], xr.at[5])
    out[1, :, lane_d] = out[1, :, lane_d] + yx[...]
    for i in range(3):
        arrived(byin.at[i], es.at[i], er.at[i])
    out[1, :, pl.ds(0, CROSS)] = (second + byin[0]) + (byin[1] + byin[2])
    other_half = pl.ds(pl.multiple_of(16 * (1 - k), 16), 16)
    arrived(done.at[other_half], hs.at[1], hr.at[1])
    out[0, :, lane_e] = done[:, pl.ds(0, BS)]
    out[1, :, lane_e] = done[:, pl.ds(BS, BS)]
    at_end = jnp.where(c == 15, 1.0, 0.0).astype(F32)
    tail = pl.ds(COLS - 2 * BS, 2 * BS)
    out[1, :, tail] = out[1, :, tail] + at_end * done[:, pl.ds(2 * BS, 2 * BS)]
    for copy in sent:
        copy.wait_send()

    @pl.when(r == 7)
    def _():
        for d in range(7):
            remote(last, own_q, qs.at[d], qr.at[0], (d, c)).wait_send()

    @pl.when(off_diagonal)
    def _():
        for level in range(2):
            for h in range(2):
                across(level, h).wait_send()

    @pl.when(diagonal)
    def _():
        for level in range(2):
            across_chip(level).wait_send()


def local(window, pattern, row_lists, factor, diag_inverse):
    dma = pltpu.SemaphoreType.DMA
    hbm = pl.BlockSpec(memory_space=pl.ANY)
    vmem = pl.BlockSpec(memory_space=pltpu.VMEM)
    smem = pl.BlockSpec(memory_space=pltpu.SMEM)
    v = lambda *shape: pltpu.VMEM(shape, F32)
    h = lambda *shape: pltpu.VMEM(shape, BF16)
    both_levels = pl.pallas_call(
        kernel,
        out_shape=jax.ShapeDtypeStruct((2, 32, COLS + BS), F32),
        in_specs=[vmem, smem, hbm, hbm, vmem],
        out_specs=vmem,
        scratch_shapes=[
            v(2, 16, 16, ROWS), v(2, 8, 2, 16, COLS), v(8, 2, 16, 2 * BS), v(ROWS, COLS), h(ROWS, COLS), h(ROWS, COLS),
            h(256, ROWS), h(256, ROWS), v(2, 2, ROWS), v(2, 2, COLS), v(256, 2 * COLS), v(256, COLS),
            h(256, COLS), h(256, COLS), h(256, COLS), h(256, COLS), h(256, COLS), h(256, COLS), v(256, 256),
            v(4, 32, COLS), v(3, 32, COLS), v(32, COLS), v(32, COLS), v(16, COLS), v(16, COLS),
            v(2, 3, 32, COLS - CROSS), v(32, COLS - CROSS), v(32, COLS - CROSS), v(4, 32, CROSS), v(3, 32, CROSS), v(3, 32, CROSS),
            v(8, 2, 16, SMALL), v(8, 16, SMALL), v(8, 16, SMALL), v(7, 16, SMALL), v(8, 16, SMALL), v(32, SMALL),
            dma((2, 9)), dma((2, 9)), dma((2, 9)), dma((2, 9)), dma((2, 8)), dma((2, 8)), dma((2, 2)), dma((2, 2)),
            dma((15,)), dma((8,)), dma((1,)), dma((1,)), dma((RB // 2,)), dma((6,)),
            dma((6,)), dma((6,)), dma((5, 4)), dma((5, 4)), dma((8,)), dma((8,)), dma((2,)), dma((2,)),
            dma((4,)), dma((4,)), dma((3,)), dma((3,)), dma((8,)), dma((8,)),
        ],
        compiler_params=pltpu.CompilerParams(
            collective_id=0, has_side_effects=True, vmem_limit_bytes=63 * 1024 * 1024
        ),
        name="selected_inversion",
    )(row_lists, jnp.swapaxes(pattern, 0, 1), window, jnp.swapaxes(factor, 1, 2), diag_inverse)
    return jnp.swapaxes(both_levels[:, :, :COLS], 1, 2), jnp.swapaxes(both_levels[:, :, COLS:], 1, 2)


def solution(mesh):
    in_specs = (P("prow", "pcol"), P("prow", "pcol"), P(), P(None, "prow", "pcol"), P())
    out_specs = (P(None, "pcol", "prow"), P(None, None, "prow"))
    return jax.shard_map(local, mesh=mesh, in_specs=in_specs, out_specs=out_specs, check_vma=False)
```

```python
import jax
import jax.numpy as jnp
from jax import lax
from jax.experimental import pallas as pl
from jax.experimental.pallas import tpu as pltpu
from jax.sharding import PartitionSpec as P

BS = 128
NB = 160
RB = 20
CB = 10
ROWS = RB * BS
COLS = CB * BS
SMALL = 512
CROSS = 6 * BS
MESH = pl.DeviceIdType.MESH
F32 = jnp.float32
BF16 = jnp.bfloat16


def remote(src, dst, send, recv, device):
    return pltpu.make_async_remote_copy(
        src_ref=src, dst_ref=dst, send_sem=send, recv_sem=recv, device_id=device, device_id_type=MESH
    )


def coords():
    r = lax.axis_index("prow")
    c = lax.axis_index("pcol")
    return r, c, r // 4, r % 4, c // 8, (c // 2) % 4, c % 2


class PairRing:
    def __init__(self, send, recv, block, half, device, p, y, sent):
        self.s, self.r, self.block, self.half, self.device = send, recv, block, half, device
        self.p, self.y, self.sent = p, y, sent
        self.q = 1 - p
        self.right, self.left, self.far = (y + 1) % 4, (y + 3) % 4, (y + 2) % 4

    def push(self, k, src, dst, device):
        copy = remote(src, dst, self.s.at[k], self.r.at[k], device)
        copy.start()
        self.sent.append(copy)

    def wait(self, k, ref):
        remote(ref, ref, self.s.at[k], self.r.at[k], self.device(self.p, self.right)).wait_recv()

    def start_pair(self, src):
        self.push(0, src, self.block(self.p, self.y), self.device(self.q, self.y))

    def start_ring(self, src):
        own = self.block(self.p, self.y)
        self.push(1, src, own, self.device(self.p, self.right))
        self.push(2, src, own, self.device(self.p, self.left))

    def from_left(self, own):
        k, p = (1, self.p) if own else (5, self.q)
        self.wait(k, self.block(p, self.left))
        part = self.half(p, self.left, 0)
        self.push(k + 2, part, part, self.device(self.p, self.right))

    def from_right(self, own):
        k, p = (2, self.p) if own else (6, self.q)
        self.wait(k, self.block(p, self.right))
        part = self.half(p, self.right, 1)
        self.push(k + 2, part, part, self.device(self.p, self.left))

    def from_pair(self):
        other = self.block(self.q, self.y)
        self.wait(0, other)
        self.push(5, other, other, self.device(self.p, self.right))
        self.push(6, other, other, self.device(self.p, self.left))

    def from_far(self, own):
        k, p = (3, self.p) if own else (7, self.q)
        self.wait(k, self.half(p, self.far, 0))
        self.wait(k + 1, self.half(p, self.far, 1))


def split(x):
    hi = x.astype(BF16)
    return hi, (x - hi.astype(F32)).astype(BF16)


def dot3(a, b, nt=False):
    dims = (((1,), (1 if nt else 0,)), ((), ()))
    (ah, al), (bh, bl) = a, b
    one = lambda u, v: lax.dot_general(u, v, dims, preferred_element_type=F32)
    return one(ah, bh) + (one(ah, bl) + one(al, bh))


def kernel(
    rl_ref, pat, w_ref, f_ref, d_ref, out,
    fr, fc, q_ref, w_all, wh, wl, fh, fl, mr, mc, x_ref, x1, ch, cl, c0h, c0l, ph, pw, acc,
    ax, asum, al, ar, ahl, ahr, yin, yx, fin, bx, bsum, byin, small, core, mine, rows_in, parts, done,
    as_, ar_, bs, br, cs, cr, ts, tr, qs, qr, ks, kr, wsem, local_sem,
    xs, xr, rs, rr, ss, sr, hs, hr, gs, gr, es, er, us, ur,
):
    r, c, xl, y, xh, z, k = coords()
    cc = c // 2
    other = c + 1 - 2 * k
    partner = (r, other)
    to_row = xh * 4 + (y + z) % 4
    got = xl * 4 + (y + 4 - z) % 4
    diagonal = jnp.logical_and(xl == xh, jnp.logical_and(y == 0, z == 0))
    off_diagonal = jnp.logical_not(diagonal)
    barrier = pltpu.get_barrier_semaphore()

    def greet(device):
        pl.semaphore_signal(barrier, inc=1, device_id=device, device_id_type=MESH)

    @pl.when(off_diagonal)
    def _():
        for h in range(2):
            greet((to_row, 2 * r + h))
            greet((cc, 2 * got + h))

    for d in range(1, 8):
        greet((r, ((cc + d) % 8) * 2 + k))
        greet(((r + d) % 8, c))
    greet(partner)

    def w_copy(i):
        rows = pl.ds(i * 2 * BS, 2 * BS)
        return pltpu.make_async_copy(w_ref.at[rows], w_all.at[rows], wsem.at[i])

    for i in range(RB // 2):
        w_copy(i).start()

    def mark(dst, first):
        def body(b, carry):
            lanes = pl.ds(pl.multiple_of(b * BS, BS), BS)
            for level in range(2):
                hit = jnp.where(rl_ref[level] == first + b, 1.0, 0.0).astype(F32)
                dst[level, :, lanes] = jnp.broadcast_to(jnp.max(hit, axis=1, keepdims=True), (2, BS))
            return carry

        return body


    @pl.when(off_diagonal)
    def _():
        pl.semaphore_wait(barrier, 19)

    @pl.when(diagonal)
    def _():
        pl.semaphore_wait(barrier, 15)

    sent = []

    def push(src, dst, send, recv, device):
        copy = remote(src, dst, send, recv, device)
        copy.start()
        sent.append(copy)

    def arrived(ref, send, recv):
        remote(ref, ref, send, recv, partner).wait_recv()

    def row_gather(level):
        return PairRing(
            as_.at[level], ar_.at[level],
            lambda p, w: fr.at[level, p * 8 + w * 2 + k],
            lambda p, w, h: fr.at[level, p * 8 + w * 2 + k, pl.ds(8 * h, 8)],
            lambda p, w: (r, p * 8 + w * 2 + k),
            xh, z, sent,
        )

    def column_gather(level):
        return PairRing(
            bs.at[level], br.at[level],
            lambda p, w: fc.at[level, p * 4 + (w + 4 - z) % 4],
            lambda p, w, h: fc.at[level, p * 4 + (w + 4 - z) % 4, h],
            lambda p, w: (p * 4 + w, c),
            xl, y, sent,
        )

    ga = [row_gather(0), row_gather(1)]
    gb = [column_gather(0), column_gather(1)]

    def across(level, h):
        return remote(
            f_ref.at[level, :, pl.ds(h * COLS, COLS)], fc.at[level, cc, k], ts.at[level, h], tr.at[level, k],
            (to_row, 2 * r + h),
        )

    def across_chip(level):
        return remote(
            f_ref.at[level, :, pl.ds((1 - k) * COLS, COLS)], fc.at[level, cc, k], ts.at[level, 0], tr.at[level, k],
            partner,
        )

    def across_own(level):
        return pltpu.make_async_copy(
            f_ref.at[level, :, pl.ds(k * COLS, COLS)], fc.at[level, cc, k], local_sem.at[2 + level]
        )

    @pl.when(off_diagonal)
    def _():
        for level in range(2):
            for h in range(2):
                across(level, h).start()

    @pl.when(diagonal)
    def _():
        for level in range(2):
            across_chip(level).start()
            across_own(level).start()

    last = f_ref.at[1, :, pl.ds(ROWS - 2 * BS, 2 * BS)]
    own_q = q_ref.at[cc, k]

    @pl.when(r == 7)
    def _():
        pltpu.make_async_copy(last, own_q, local_sem.at[0]).start()
        for d in range(7):
            remote(last, own_q, qs.at[d], qr.at[0], (d, c)).start()

    own_copy = [pltpu.make_async_copy(f_ref.at[level], fr.at[level, c], local_sem.at[4 + level]) for level in range(2)]
    for copy in own_copy:
        copy.start()

    def swap(level, chip, src=None):
        block = fr.at[level, chip * 2 + k]
        push(block if src is None else src, block, cs.at[level, chip], cr.at[level, chip], partner)

    right, left, far = (z + 1) % 4, (z + 3) % 4, (z + 2) % 4
    chip = lambda p, w: p * 4 + w

    def row_step(level, step, own):
        side = xh if own else 1 - xh
        if step == "left":
            ga[level].from_left(own)
            swap(level, chip(side, left))
        elif step == "right":
            ga[level].from_right(own)
            swap(level, chip(side, right))
        elif step == "far":
            ga[level].from_far(own)
            swap(level, chip(side, far))
        else:
            ga[level].from_pair()
            swap(level, chip(1 - xh, z))

    def column_start(level):
        @pl.when(off_diagonal)
        def _():
            for h in range(2):
                arrived(fc.at[level, got, h], ts.at[level, h], tr.at[level, h])

        @pl.when(diagonal)
        def _():
            arrived(fc.at[level, got, 1 - k], ts.at[level, 0], tr.at[level, 1 - k])
            across_own(level).wait()

        gb[level].start_pair(fc.at[level, got])
        gb[level].start_ring(fc.at[level, got])

    def split_window(i0, i1):
        for i in range(i0, i1):
            w_copy(i).wait()

        def body(i, carry):
            rows = pl.ds(pl.multiple_of(i * BS, BS), BS)
            row_ok = jnp.where(r * RB + i < NB - 2, 1, 0)
            for j in range(CB):
                lanes = pl.ds(j * BS, BS)
                ok = jnp.where(c * CB + j < NB - 2, 1, 0)
                keep = (pat[j, i] * row_ok * ok).astype(F32)
                wh[rows, lanes], wl[rows, lanes] = split(w_all[rows, lanes] * keep)
            return carry

        lax.fori_loop(2 * i0, 2 * i1, body, 0)

    def split_rows(level):
        def body(b, carry):
            lanes = pl.ds(pl.multiple_of(b * BS, BS), BS)
            for s in range(2):
                rows = pl.ds(s * BS, BS)
                block = fr[level, pl.ds(8 * s, 8), :, lanes].reshape(BS, BS) * mr[level, pl.ds(s, 1), lanes]
                fh[rows, lanes], fl[rows, lanes] = split(block)
            return carry

        lax.fori_loop(0, RB, body, 0)

    def product(n):
        acc[...] = jnp.zeros((256, 256), F32)
        lanes = pl.ds(n * 256, 256)

        def body(i, carry):
            depth = pl.ds(pl.multiple_of(i * 1280, 1280), 1280)
            acc[...] += dot3((fh[:, depth], fl[:, depth]), (wh[depth, lanes], wl[depth, lanes]))
            return carry

        lax.fori_loop(0, ROWS // 1280, body, 0)

    def first_level(n):
        product(n)
        lanes = pl.ds(n * 256, 256)
        for s in range(2):
            rows = pl.ds(s * BS, BS)
            x_ref[rows, lanes] = -(acc[rows, :] * mc[0, pl.ds(s, 1), lanes])

    def second_level(n):
        product(n)
        x1[:, pl.ds(n * 256, 256)] = acc[...]

    def q_spread():
        @pl.when(r == 7)
        def _():
            pltpu.make_async_copy(last, own_q, local_sem.at[0]).wait()

        @pl.when(r != 7)
        def _():
            arrived(own_q, qs.at[0], qr.at[0])

        for d in range(1, 8):
            push(own_q, own_q, qs.at[7 + d], qr.at[d], (r, ((cc + d) % 8) * 2 + k))

    def q_swap():
        for d in range(1, 8):
            arrived(q_ref.at[(cc + 8 - d) % 8, k], qs.at[0], qr.at[d])
        half = q_ref.at[:, k]
        push(half, half, ks.at[0], kr.at[0], partner)

    def swapped(level):
        for m in range(8):
            arrived(fr.at[level, m * 2 + 1 - k], cs.at[level, m], cr.at[level, m])
        own_copy[level].wait()

    ga[0].start_pair(f_ref.at[0])
    ga[0].start_ring(f_ref.at[0])
    ga[1].start_pair(f_ref.at[1])
    for level in range(2):
        swap(level, cc, f_ref.at[level])
    lax.fori_loop(0, RB, mark(mr, r * RB), 0)
    row_step(0, "left", True)
    row_step(0, "right", True)
    q_spread()
    row_step(0, "pair", True)
    split_window(0, 4)
    column_start(0)
    column_start(1)
    row_step(0, "far", True)
    lax.fori_loop(0, CB, mark(mc, c * CB), 0)
    row_step(0, "left", False)
    row_step(0, "right", False)
    ga[1].start_ring(f_ref.at[1])
    row_step(1, "pair", True)
    split_window(4, 7)
    q_swap()
    gb[0].from_left(True)
    gb[0].from_right(True)
    row_step(0, "far", False)
    split_window(7, 10)
    gb[0].from_pair()
    gb[1].from_pair()
    swapped(0)

    split_rows(0)
    first_level(0)
    gb[1].from_left(True)
    gb[1].from_right(True)
    row_step(1, "left", True)
    row_step(1, "right", True)
    first_level(1)
    first_level(2)
    gb[0].from_far(True)
    row_step(1, "far", True)
    row_step(1, "left", False)
    row_step(1, "right", False)
    first_level(3)
    first_level(4)

    px = (4 * (1 - xl) + y, c)
    yright, yleft, yfar = (y + 1) % 4, (y + 3) % 4, (y + 2) % 4
    dr, dl = (4 * xl + yright, c), (4 * xl + yleft, c)

    def rows_of(p, w, h=None):
        if h is None:
            return pl.ds(pl.multiple_of((4 * p + w) * 32, 32), 32)
        return pl.ds(pl.multiple_of((4 * p + w) * 32 + 16 * h, 16), 16)

    lane_a = pl.ds(0, COLS)
    lane_c = pl.ds(COLS + CROSS, COLS - CROSS)
    lane_b = pl.ds(COLS, CROSS)
    dfar = (4 * xl + yfar, c)
    along = ((0, yright, dr), (1, yleft, dl), (2, yfar, dfar))

    def spread(p, v):
        for i, w, device in along:
            push(x_ref.at[rows_of(p, w), lane_c], yin.at[v, i], rs.at[v, i], rr.at[v, i], device)

    def collect(p, v):
        for i in range(3):
            arrived(yin.at[v, i], rs.at[v, i], rr.at[v, i])
        return (x_ref[rows_of(p, y), lane_c] + yin[v, 0]) + (yin[v, 1] + yin[v, 2])

    q = 1 - xl
    for w, d in ((0, yfar), (1, yright), (2, yleft), (3, y)):
        push(x_ref.at[rows_of(q, d), lane_a], ax.at[w], xs.at[w], xr.at[w], px)

    gb[0].from_left(False)
    gb[0].from_right(False)
    gb[1].from_far(True)
    gb[1].from_left(False)
    gb[1].from_right(False)
    row_step(1, "far", False)
    swapped(1)
    split_rows(1)
    second_level(0)
    arrived(ax.at[0], xs.at[0], xr.at[0])
    asum[0] = x_ref[rows_of(xl, yfar), lane_a] + ax[0]
    push(asum.at[0, pl.ds(0, 16)], ahl, rs.at[4, 0], rr.at[4, 0], dr)
    push(asum.at[0, pl.ds(16, 16)], ahr, rs.at[4, 1], rr.at[4, 1], dl)
    second_level(1)
    gb[0].from_far(False)
    second_level(2)
    arrived(ax.at[1], xs.at[1], xr.at[1])
    asum[1] = x_ref[rows_of(xl, yright), lane_a] + ax[1]
    arrived(ahl, rs.at[4, 0], rr.at[4, 0])
    asum[1, pl.ds(0, 16)] = asum[1, pl.ds(0, 16)] + ahl[...]
    push(asum.at[1], al, rs.at[4, 2], rr.at[4, 2], dr)
    second_level(3)
    arrived(ax.at[2], xs.at[2], xr.at[2])
    asum[2] = x_ref[rows_of(xl, yleft), lane_a] + ax[2]
    arrived(ahr, rs.at[4, 1], rr.at[4, 1])
    asum[2, pl.ds(16, 16)] = asum[2, pl.ds(16, 16)] + ahr[...]
    push(asum.at[2], ar, rs.at[4, 3], rr.at[4, 3], dl)
    second_level(4)

    half = q_ref.at[:, 1 - k]
    arrived(half, ks.at[0], kr.at[0])
    qv = split(q_ref[...].reshape(256, 256))
    ph[...], pw[...] = split(x_ref[:, lane_a])
    def second_sum(n, carry):
        lanes = pl.ds(pl.multiple_of(n * 256, 256), 256)
        full = x1[:, lanes] + dot3(qv, (ph[:, lanes], pw[:, lanes]))
        out = pl.ds(pl.multiple_of(COLS + n * 256, 256), 256)
        for s in range(2):
            x_ref[pl.ds(s * BS, BS), out] = -(full[s * BS:(s + 1) * BS] * mc[1, pl.ds(s, 1), lanes])
        return carry

    lax.fori_loop(0, CB // 2, second_sum, 0)
    spread(q, 0)
    for w, d in ((0, yfar), (1, yright), (2, yleft), (3, y)):
        push(x_ref.at[rows_of(q, d), lane_b], bx.at[w], gs.at[w], gr.at[w], px)
    spread(xl, 1)

    gb[1].from_far(False)
    for s in range(2):
        rows = pl.ds(s * BS, BS)

        def body(j, carry):
            lanes = pl.ds(pl.multiple_of(j * BS, BS), BS)
            block = fc[1, pl.ds(4 * s, 4), :, :, lanes].reshape(BS, BS) * mc[1, pl.ds(s, 1), lanes]
            ch[rows, lanes], cl[rows, lanes] = split(block)
            block = fc[0, pl.ds(4 * s, 4), :, :, lanes].reshape(BS, BS)
            c0h[rows, lanes], c0l[rows, lanes] = split(block)
            return carry

        lax.fori_loop(0, CB, body, 0)
    pair = lambda h, l, rows: (h[rows, :], l[rows, :])
    whole = pl.ds(0, 256)
    a_t = dot3(pair(ch, cl, whole), pair(ph, pw, whole), nt=True)
    chosen = jnp.where(jnp.logical_and(r == 0, c == 0), 1.0, 0.0).astype(F32)
    s_t = []
    for s in range(2):
        rows = pl.ds(s * BS, BS)
        s_t.append(chosen * d_ref[0, :, rows] - dot3(pair(ph, pw, rows), pair(c0h, c0l, rows), nt=True))
    slot = a_t + jnp.concatenate(
        [dot3((qv[0][:, s * BS:(s + 1) * BS], qv[1][:, s * BS:(s + 1) * BS]), split(s_t[s])) for s in range(2)], axis=1
    )
    a_s, slot_s = split(a_t), split(slot)
    for s in range(2):
        rows = pl.ds(s * BS, BS)
        cut = lambda v: (v[0][s * BS:(s + 1) * BS], v[1][s * BS:(s + 1) * BS])
        second = (
            chosen * d_ref[1, :, rows]
            + dot3(split(x1[rows, :]), pair(ch, cl, rows), nt=True)
            + dot3(cut(qv), cut(a_s), nt=True)
            + dot3(cut(slot_s), cut(qv), nt=True)
        )
        for lanes, value in (
            (pl.ds(0, BS), s_t[s]), (pl.ds(BS, BS), second), (pl.ds(2 * BS, 2 * BS), -slot[s * BS:(s + 1) * BS])
        ):
            small[pl.ds(4 * s, 4), :, :, lanes] = value.reshape(4, 2, 16, value.shape[1])
    theirs = small.at[:, 1 - k]
    push(theirs, core, hs.at[0], hr.at[0], partner)

    def crossed(w, i, d, device):
        arrived(bx.at[w], gs.at[w], gr.at[w])
        bsum[i] = x_ref[rows_of(xl, d), lane_b] + bx[w]
        push(bsum.at[i], byin.at[i], es.at[i], er.at[i], device)

    arrived(core, hs.at[0], hr.at[0])
    mine[...] = small[:, k] + core[...]
    for d in range(1, 8):
        to = (r + d) % 8
        push(mine.at[to], rows_in.at[d - 1], us.at[d], ur.at[d], (to, c))
    crossed(0, 2, yfar, dfar)
    crossed(1, 0, yright, dr)
    crossed(2, 1, yleft, dl)
    total = mine[r]
    for d in range(1, 8):
        arrived(rows_in.at[d - 1], us.at[d], ur.at[d])
        total = total + rows_in[d - 1]
    parts[cc] = total
    for d in range(1, 8):
        push(parts.at[cc], parts.at[cc], ss.at[d], sr.at[d], (r, ((cc + d) % 8) * 2 + k))
    fin[...] = collect(q, 0)
    push(fin, yx, xs.at[5], xr.at[5], px)

    arrived(ax.at[3], xs.at[3], xr.at[3])
    first = x_ref[rows_of(xl, y), lane_a] + ax[3]
    arrived(al, rs.at[4, 2], rr.at[4, 2])
    arrived(ar, rs.at[4, 3], rr.at[4, 3])
    out[0, :, lane_a] = first + (al[...] + ar[...])

    own_half = pl.ds(pl.multiple_of(16 * k, 16), 16)
    for d in range(1, 8):
        arrived(parts.at[(cc + 8 - d) % 8], ss.at[d], sr.at[d])
    total = parts[0]
    for d in range(1, 8):
        total = total + parts[d]
    done[own_half, :] = total
    push(done.at[own_half], done.at[own_half], hs.at[1], hr.at[1], partner)

    lane_d = pl.ds(CROSS, COLS - CROSS)
    lane_e = pl.ds(COLS, BS)
    out[1, :, lane_d] = collect(xl, 1)
    arrived(bx.at[3], gs.at[3], gr.at[3])
    second = x_ref[rows_of(xl, y), lane_b] + bx[3]
    arrived(yx, xs.at[5], xr.at[5])
    out[1, :, lane_d] = out[1, :, lane_d] + yx[...]
    for i in range(3):
        arrived(byin.at[i], es.at[i], er.at[i])
    out[1, :, pl.ds(0, CROSS)] = (second + byin[0]) + (byin[1] + byin[2])
    other_half = pl.ds(pl.multiple_of(16 * (1 - k), 16), 16)
    arrived(done.at[other_half], hs.at[1], hr.at[1])
    out[0, :, lane_e] = done[:, pl.ds(0, BS)]
    out[1, :, lane_e] = done[:, pl.ds(BS, BS)]
    at_end = jnp.where(c == 15, 1.0, 0.0).astype(F32)
    tail = pl.ds(COLS - 2 * BS, 2 * BS)
    out[1, :, tail] = out[1, :, tail] + at_end * done[:, pl.ds(2 * BS, 2 * BS)]
    for copy in sent:
        copy.wait_send()

    @pl.when(r == 7)
    def _():
        for d in range(7):
            remote(last, own_q, qs.at[d], qr.at[0], (d, c)).wait_send()

    @pl.when(off_diagonal)
    def _():
        for level in range(2):
            for h in range(2):
                across(level, h).wait_send()

    @pl.when(diagonal)
    def _():
        for level in range(2):
            across_chip(level).wait_send()


def part_kernel(both_ref, panels, diagonals):
    panels[...] = both_ref[:, :, pl.ds(0, COLS)]
    diagonals[...] = both_ref[:, :, pl.ds(COLS, BS)]


def local(window, pattern, row_lists, factor, diag_inverse):
    dma = pltpu.SemaphoreType.DMA
    hbm = pl.BlockSpec(memory_space=pl.ANY)
    vmem = pl.BlockSpec(memory_space=pltpu.VMEM)
    smem = pl.BlockSpec(memory_space=pltpu.SMEM)
    v = lambda *shape: pltpu.VMEM(shape, F32)
    h = lambda *shape: pltpu.VMEM(shape, BF16)
    both_levels = pl.pallas_call(
        kernel,
        out_shape=jax.ShapeDtypeStruct((2, 32, COLS + BS), F32),
        in_specs=[vmem, smem, hbm, hbm, vmem],
        out_specs=vmem,
        scratch_shapes=[
            v(2, 16, 16, ROWS), v(2, 8, 2, 16, COLS), v(8, 2, 16, 2 * BS), v(ROWS, COLS), h(ROWS, COLS), h(ROWS, COLS),
            h(256, ROWS), h(256, ROWS), v(2, 2, ROWS), v(2, 2, COLS), v(256, 2 * COLS), v(256, COLS),
            h(256, COLS), h(256, COLS), h(256, COLS), h(256, COLS), h(256, COLS), h(256, COLS), v(256, 256),
            v(4, 32, COLS), v(3, 32, COLS), v(32, COLS), v(32, COLS), v(16, COLS), v(16, COLS),
            v(2, 3, 32, COLS - CROSS), v(32, COLS - CROSS), v(32, COLS - CROSS), v(4, 32, CROSS), v(3, 32, CROSS), v(3, 32, CROSS),
            v(8, 2, 16, SMALL), v(8, 16, SMALL), v(8, 16, SMALL), v(7, 16, SMALL), v(8, 16, SMALL), v(32, SMALL),
            dma((2, 9)), dma((2, 9)), dma((2, 9)), dma((2, 9)), dma((2, 8)), dma((2, 8)), dma((2, 2)), dma((2, 2)),
            dma((15,)), dma((8,)), dma((1,)), dma((1,)), dma((RB // 2,)), dma((6,)),
            dma((6,)), dma((6,)), dma((5, 4)), dma((5, 4)), dma((8,)), dma((8,)), dma((2,)), dma((2,)),
            dma((4,)), dma((4,)), dma((3,)), dma((3,)), dma((8,)), dma((8,)),
        ],
        compiler_params=pltpu.CompilerParams(
            collective_id=0, has_side_effects=True, vmem_limit_bytes=63 * 1024 * 1024
        ),
        name="selected_inversion",
    )(row_lists, jnp.swapaxes(pattern, 0, 1), window, jnp.swapaxes(factor, 1, 2), diag_inverse)
    panels, diagonals = pl.pallas_call(
        part_kernel,
        out_shape=(jax.ShapeDtypeStruct((2, 32, COLS), F32), jax.ShapeDtypeStruct((2, 32, BS), F32)),
        in_specs=[vmem],
        out_specs=(vmem, vmem),
        name="parts",
    )(both_levels)
    return jnp.swapaxes(panels, 1, 2), jnp.swapaxes(diagonals, 1, 2)


def solution(mesh):
    in_specs = (P("prow", "pcol"), P("prow", "pcol"), P(), P(None, "prow", "pcol"), P())
    out_specs = (P(None, "pcol", "prow"), P(None, None, "prow"))
    return jax.shard_map(local, mesh=mesh, in_specs=in_specs, out_specs=out_specs, check_vma=False)
```

```python
import jax
import jax.numpy as jnp
from jax import lax
from jax.experimental import pallas as pl
from jax.experimental.pallas import tpu as pltpu
from jax.sharding import PartitionSpec as P

BS = 128
NB = 160
RB = 20
CB = 10
ROWS = RB * BS
COLS = CB * BS
SMALL = 512
CROSS = 6 * BS
MESH = pl.DeviceIdType.MESH
F32 = jnp.float32
BF16 = jnp.bfloat16


def remote(src, dst, send, recv, device):
    return pltpu.make_async_remote_copy(
        src_ref=src, dst_ref=dst, send_sem=send, recv_sem=recv, device_id=device, device_id_type=MESH
    )


def coords():
    r = lax.axis_index("prow")
    c = lax.axis_index("pcol")
    return r, c, r // 4, r % 4, c // 8, (c // 2) % 4, c % 2


class PairRing:
    def __init__(self, send, recv, block, half, device, p, y, sent):
        self.s, self.r, self.block, self.half, self.device = send, recv, block, half, device
        self.p, self.y, self.sent = p, y, sent
        self.q = 1 - p
        self.right, self.left, self.far = (y + 1) % 4, (y + 3) % 4, (y + 2) % 4

    def push(self, k, src, dst, device):
        copy = remote(src, dst, self.s.at[k], self.r.at[k], device)
        copy.start()
        self.sent.append(copy)

    def wait(self, k, ref):
        remote(ref, ref, self.s.at[k], self.r.at[k], self.device(self.p, self.right)).wait_recv()

    def start_pair(self, src):
        self.push(0, src, self.block(self.p, self.y), self.device(self.q, self.y))

    def start_ring(self, src):
        own = self.block(self.p, self.y)
        self.push(1, src, own, self.device(self.p, self.right))
        self.push(2, src, own, self.device(self.p, self.left))

    def from_left(self, own):
        k, p = (1, self.p) if own else (5, self.q)
        self.wait(k, self.block(p, self.left))
        part = self.half(p, self.left, 0)
        self.push(k + 2, part, part, self.device(self.p, self.right))

    def from_right(self, own):
        k, p = (2, self.p) if own else (6, self.q)
        self.wait(k, self.block(p, self.right))
        part = self.half(p, self.right, 1)
        self.push(k + 2, part, part, self.device(self.p, self.left))

    def from_pair(self):
        other = self.block(self.q, self.y)
        self.wait(0, other)
        self.push(5, other, other, self.device(self.p, self.right))
        self.push(6, other, other, self.device(self.p, self.left))

    def from_far(self, own):
        k, p = (3, self.p) if own else (7, self.q)
        self.wait(k, self.half(p, self.far, 0))
        self.wait(k + 1, self.half(p, self.far, 1))


def split(x):
    hi = x.astype(BF16)
    return hi, (x - hi.astype(F32)).astype(BF16)


def dot3(a, b, nt=False):
    dims = (((1,), (1 if nt else 0,)), ((), ()))
    (ah, al), (bh, bl) = a, b
    one = lambda u, v: lax.dot_general(u, v, dims, preferred_element_type=F32)
    return one(ah, bh) + (one(ah, bl) + one(al, bh))


def kernel(
    rl_ref, pat, w_ref, f_ref, d_ref, out,
    fr, fc, q_ref, w_all, wh, wl, fh, fl, mr, mc, x_ref, x1, ch, cl, c0h, c0l, ph, pw, acc,
    ax, asum, al, ar, ahl, ahr, yin, yx, fin, bx, bsum, byin, small, core, mine, rows_in, parts, done,
    as_, ar_, bs, br, cs, cr, ts, tr, qs, qr, ks, kr, wsem, local_sem,
    xs, xr, rs, rr, ss, sr, hs, hr, gs, gr, es, er, us, ur,
):
    r, c, xl, y, xh, z, k = coords()
    cc = c // 2
    other = c + 1 - 2 * k
    partner = (r, other)
    to_row = xh * 4 + (y + z) % 4
    got = xl * 4 + (y + 4 - z) % 4
    diagonal = jnp.logical_and(xl == xh, jnp.logical_and(y == 0, z == 0))
    off_diagonal = jnp.logical_not(diagonal)
    barrier = pltpu.get_barrier_semaphore()

    def greet(device):
        pl.semaphore_signal(barrier, inc=1, device_id=device, device_id_type=MESH)

    @pl.when(off_diagonal)
    def _():
        for h in range(2):
            greet((to_row, 2 * r + h))
            greet((cc, 2 * got + h))

    for d in range(1, 8):
        greet((r, ((cc + d) % 8) * 2 + k))
        greet(((r + d) % 8, c))
    greet(partner)

    def w_copy(i):
        rows = pl.ds(i * 2 * BS, 2 * BS)
        return pltpu.make_async_copy(w_ref.at[rows], w_all.at[rows], wsem.at[i])

    for i in range(RB // 2):
        w_copy(i).start()

    def mark(dst, first):
        def body(b, carry):
            lanes = pl.ds(pl.multiple_of(b * BS, BS), BS)
            for level in range(2):
                hit = jnp.where(rl_ref[level] == first + b, 1.0, 0.0).astype(F32)
                dst[level, :, lanes] = jnp.broadcast_to(jnp.max(hit, axis=1, keepdims=True), (2, BS))
            return carry

        return body


    @pl.when(off_diagonal)
    def _():
        pl.semaphore_wait(barrier, 19)

    @pl.when(diagonal)
    def _():
        pl.semaphore_wait(barrier, 15)

    sent = []

    def push(src, dst, send, recv, device):
        copy = remote(src, dst, send, recv, device)
        copy.start()
        sent.append(copy)

    def arrived(ref, send, recv):
        remote(ref, ref, send, recv, partner).wait_recv()

    def row_gather(level):
        return PairRing(
            as_.at[level], ar_.at[level],
            lambda p, w: fr.at[level, p * 8 + w * 2 + k],
            lambda p, w, h: fr.at[level, p * 8 + w * 2 + k, pl.ds(8 * h, 8)],
            lambda p, w: (r, p * 8 + w * 2 + k),
            xh, z, sent,
        )

    def column_gather(level):
        return PairRing(
            bs.at[level], br.at[level],
            lambda p, w: fc.at[level, p * 4 + (w + 4 - z) % 4],
            lambda p, w, h: fc.at[level, p * 4 + (w + 4 - z) % 4, h],
            lambda p, w: (p * 4 + w, c),
            xl, y, sent,
        )

    ga = [row_gather(0), row_gather(1)]
    gb = [column_gather(0), column_gather(1)]

    def across(level, h):
        return remote(
            f_ref.at[level, :, pl.ds(h * COLS, COLS)], fc.at[level, cc, k], ts.at[level, h], tr.at[level, k],
            (to_row, 2 * r + h),
        )

    def across_chip(level):
        return remote(
            f_ref.at[level, :, pl.ds((1 - k) * COLS, COLS)], fc.at[level, cc, k], ts.at[level, 0], tr.at[level, k],
            partner,
        )

    def across_own(level):
        return pltpu.make_async_copy(
            f_ref.at[level, :, pl.ds(k * COLS, COLS)], fc.at[level, cc, k], local_sem.at[2 + level]
        )

    @pl.when(off_diagonal)
    def _():
        for level in range(2):
            for h in range(2):
                across(level, h).start()

    @pl.when(diagonal)
    def _():
        for level in range(2):
            across_chip(level).start()
            across_own(level).start()

    last = f_ref.at[1, :, pl.ds(ROWS - 2 * BS, 2 * BS)]
    own_q = q_ref.at[cc, k]

    @pl.when(r == 7)
    def _():
        pltpu.make_async_copy(last, own_q, local_sem.at[0]).start()
        for d in range(7):
            remote(last, own_q, qs.at[d], qr.at[0], (d, c)).start()

    own_copy = [pltpu.make_async_copy(f_ref.at[level], fr.at[level, c], local_sem.at[4 + level]) for level in range(2)]
    for copy in own_copy:
        copy.start()

    def swap(level, chip, src=None):
        block = fr.at[level, chip * 2 + k]
        push(block if src is None else src, block, cs.at[level, chip], cr.at[level, chip], partner)

    right, left, far = (z + 1) % 4, (z + 3) % 4, (z + 2) % 4
    chip = lambda p, w: p * 4 + w

    def row_step(level, step, own):
        side = xh if own else 1 - xh
        if step == "left":
            ga[level].from_left(own)
            swap(level, chip(side, left))
        elif step == "right":
            ga[level].from_right(own)
            swap(level, chip(side, right))
        elif step == "far":
            ga[level].from_far(own)
            swap(level, chip(side, far))
        else:
            ga[level].from_pair()
            swap(level, chip(1 - xh, z))

    def column_start(level):
        @pl.when(off_diagonal)
        def _():
            for h in range(2):
                arrived(fc.at[level, got, h], ts.at[level, h], tr.at[level, h])

        @pl.when(diagonal)
        def _():
            arrived(fc.at[level, got, 1 - k], ts.at[level, 0], tr.at[level, 1 - k])
            across_own(level).wait()

        gb[level].start_pair(fc.at[level, got])
        gb[level].start_ring(fc.at[level, got])

    def split_window(i0, i1):
        for i in range(i0, i1):
            w_copy(i).wait()

        def body(i, carry):
            rows = pl.ds(pl.multiple_of(i * BS, BS), BS)
            row_ok = jnp.where(r * RB + i < NB - 2, 1, 0)
            for j in range(CB):
                lanes = pl.ds(j * BS, BS)
                ok = jnp.where(c * CB + j < NB - 2, 1, 0)
                keep = (pat[j, i] * row_ok * ok).astype(F32)
                wh[rows, lanes], wl[rows, lanes] = split(w_all[rows, lanes] * keep)
            return carry

        lax.fori_loop(2 * i0, 2 * i1, body, 0)

    def split_rows(level):
        def body(b, carry):
            lanes = pl.ds(pl.multiple_of(b * BS, BS), BS)
            for s in range(2):
                rows = pl.ds(s * BS, BS)
                block = fr[level, pl.ds(8 * s, 8), :, lanes].reshape(BS, BS) * mr[level, pl.ds(s, 1), lanes]
                fh[rows, lanes], fl[rows, lanes] = split(block)
            return carry

        lax.fori_loop(0, RB, body, 0)

    def product(n):
        acc[...] = jnp.zeros((256, 256), F32)
        lanes = pl.ds(n * 256, 256)

        def body(i, carry):
            depth = pl.ds(pl.multiple_of(i * 1280, 1280), 1280)
            acc[...] += dot3((fh[:, depth], fl[:, depth]), (wh[depth, lanes], wl[depth, lanes]))
            return carry

        lax.fori_loop(0, ROWS // 1280, body, 0)

    def first_level(n):
        product(n)
        lanes = pl.ds(n * 256, 256)
        for s in range(2):
            rows = pl.ds(s * BS, BS)
            x_ref[rows, lanes] = -(acc[rows, :] * mc[0, pl.ds(s, 1), lanes])

    def second_level(n):
        product(n)
        x1[:, pl.ds(n * 256, 256)] = acc[...]

    def q_spread():
        @pl.when(r == 7)
        def _():
            pltpu.make_async_copy(last, own_q, local_sem.at[0]).wait()

        @pl.when(r != 7)
        def _():
            arrived(own_q, qs.at[0], qr.at[0])

        for d in range(1, 8):
            push(own_q, own_q, qs.at[7 + d], qr.at[d], (r, ((cc + d) % 8) * 2 + k))

    def q_swap():
        for d in range(1, 8):
            arrived(q_ref.at[(cc + 8 - d) % 8, k], qs.at[0], qr.at[d])
        half = q_ref.at[:, k]
        push(half, half, ks.at[0], kr.at[0], partner)

    def swapped(level):
        for m in range(8):
            arrived(fr.at[level, m * 2 + 1 - k], cs.at[level, m], cr.at[level, m])
        own_copy[level].wait()

    ga[0].start_pair(f_ref.at[0])
    ga[0].start_ring(f_ref.at[0])
    ga[1].start_pair(f_ref.at[1])
    for level in range(2):
        swap(level, cc, f_ref.at[level])
    lax.fori_loop(0, RB, mark(mr, r * RB), 0)
    row_step(0, "left", True)
    row_step(0, "right", True)
    q_spread()
    row_step(0, "pair", True)
    split_window(0, 4)
    column_start(0)
    column_start(1)
    row_step(0, "far", True)
    lax.fori_loop(0, CB, mark(mc, c * CB), 0)
    row_step(0, "left", False)
    row_step(0, "right", False)
    ga[1].start_ring(f_ref.at[1])
    row_step(1, "pair", True)
    split_window(4, 7)
    q_swap()
    gb[0].from_left(True)
    gb[0].from_right(True)
    row_step(0, "far", False)
    split_window(7, 10)
    gb[0].from_pair()
    gb[1].from_pair()
    swapped(0)

    split_rows(0)
    first_level(0)
    gb[1].from_left(True)
    gb[1].from_right(True)
    row_step(1, "left", True)
    row_step(1, "right", True)
    first_level(1)
    first_level(2)
    gb[0].from_far(True)
    row_step(1, "far", True)
    row_step(1, "left", False)
    row_step(1, "right", False)
    first_level(3)
    first_level(4)

    px = (4 * (1 - xl) + y, c)
    yright, yleft, yfar = (y + 1) % 4, (y + 3) % 4, (y + 2) % 4
    dr, dl = (4 * xl + yright, c), (4 * xl + yleft, c)

    def rows_of(p, w, h=None):
        if h is None:
            return pl.ds(pl.multiple_of((4 * p + w) * 32, 32), 32)
        return pl.ds(pl.multiple_of((4 * p + w) * 32 + 16 * h, 16), 16)

    lane_a = pl.ds(0, COLS)
    lane_c = pl.ds(COLS + CROSS, COLS - CROSS)
    lane_b = pl.ds(COLS, CROSS)
    dfar = (4 * xl + yfar, c)
    along = ((0, yright, dr), (1, yleft, dl), (2, yfar, dfar))

    def spread(p, v):
        for i, w, device in along:
            push(x_ref.at[rows_of(p, w), lane_c], yin.at[v, i], rs.at[v, i], rr.at[v, i], device)

    def collect(p, v):
        for i in range(3):
            arrived(yin.at[v, i], rs.at[v, i], rr.at[v, i])
        return (x_ref[rows_of(p, y), lane_c] + yin[v, 0]) + (yin[v, 1] + yin[v, 2])

    q = 1 - xl

    gb[0].from_left(False)
    gb[0].from_right(False)
    gb[1].from_far(True)
    gb[1].from_left(False)
    gb[1].from_right(False)
    for w, d in ((0, yfar), (1, yright), (2, yleft), (3, y)):
        push(x_ref.at[rows_of(q, d), lane_a], ax.at[w], xs.at[w], xr.at[w], px)
    row_step(1, "far", False)
    swapped(1)
    split_rows(1)
    second_level(0)
    arrived(ax.at[0], xs.at[0], xr.at[0])
    asum[0] = x_ref[rows_of(xl, yfar), lane_a] + ax[0]
    push(asum.at[0, pl.ds(0, 16)], ahl, rs.at[4, 0], rr.at[4, 0], dr)
    push(asum.at[0, pl.ds(16, 16)], ahr, rs.at[4, 1], rr.at[4, 1], dl)
    second_level(1)
    gb[0].from_far(False)
    second_level(2)
    arrived(ax.at[1], xs.at[1], xr.at[1])
    asum[1] = x_ref[rows_of(xl, yright), lane_a] + ax[1]
    arrived(ahl, rs.at[4, 0], rr.at[4, 0])
    asum[1, pl.ds(0, 16)] = asum[1, pl.ds(0, 16)] + ahl[...]
    push(asum.at[1], al, rs.at[4, 2], rr.at[4, 2], dr)
    second_level(3)
    arrived(ax.at[2], xs.at[2], xr.at[2])
    asum[2] = x_ref[rows_of(xl, yleft), lane_a] + ax[2]
    arrived(ahr, rs.at[4, 1], rr.at[4, 1])
    asum[2, pl.ds(16, 16)] = asum[2, pl.ds(16, 16)] + ahr[...]
    push(asum.at[2], ar, rs.at[4, 3], rr.at[4, 3], dl)
    second_level(4)

    half = q_ref.at[:, 1 - k]
    arrived(half, ks.at[0], kr.at[0])
    qv = split(q_ref[...].reshape(256, 256))
    ph[...], pw[...] = split(x_ref[:, lane_a])
    def second_sum(n, carry):
        lanes = pl.ds(pl.multiple_of(n * 256, 256), 256)
        full = x1[:, lanes] + dot3(qv, (ph[:, lanes], pw[:, lanes]))
        out = pl.ds(pl.multiple_of(COLS + n * 256, 256), 256)
        for s in range(2):
            x_ref[pl.ds(s * BS, BS), out] = -(full[s * BS:(s + 1) * BS] * mc[1, pl.ds(s, 1), lanes])
        return carry

    lax.fori_loop(0, CB // 2, second_sum, 0)
    spread(q, 0)
    for w, d in ((0, yfar), (1, yright), (2, yleft), (3, y)):
        push(x_ref.at[rows_of(q, d), lane_b], bx.at[w], gs.at[w], gr.at[w], px)
    spread(xl, 1)

    gb[1].from_far(False)
    for s in range(2):
        rows = pl.ds(s * BS, BS)

        def body(j, carry):
            lanes = pl.ds(pl.multiple_of(j * BS, BS), BS)
            block = fc[1, pl.ds(4 * s, 4), :, :, lanes].reshape(BS, BS) * mc[1, pl.ds(s, 1), lanes]
            ch[rows, lanes], cl[rows, lanes] = split(block)
            block = fc[0, pl.ds(4 * s, 4), :, :, lanes].reshape(BS, BS)
            c0h[rows, lanes], c0l[rows, lanes] = split(block)
            return carry

        lax.fori_loop(0, CB, body, 0)
    pair = lambda h, l, rows: (h[rows, :], l[rows, :])
    whole = pl.ds(0, 256)
    a_t = dot3(pair(ch, cl, whole), pair(ph, pw, whole), nt=True)
    chosen = jnp.where(jnp.logical_and(r == 0, c == 0), 1.0, 0.0).astype(F32)
    s_t = []
    for s in range(2):
        rows = pl.ds(s * BS, BS)
        s_t.append(chosen * d_ref[0, :, rows] - dot3(pair(ph, pw, rows), pair(c0h, c0l, rows), nt=True))
    slot = a_t + jnp.concatenate(
        [dot3((qv[0][:, s * BS:(s + 1) * BS], qv[1][:, s * BS:(s + 1) * BS]), split(s_t[s])) for s in range(2)], axis=1
    )
    a_s, slot_s = split(a_t), split(slot)
    for s in range(2):
        rows = pl.ds(s * BS, BS)
        cut = lambda v: (v[0][s * BS:(s + 1) * BS], v[1][s * BS:(s + 1) * BS])
        second = (
            chosen * d_ref[1, :, rows]
            + dot3(split(x1[rows, :]), pair(ch, cl, rows), nt=True)
            + dot3(cut(qv), cut(a_s), nt=True)
            + dot3(cut(slot_s), cut(qv), nt=True)
        )
        for lanes, value in (
            (pl.ds(0, BS), s_t[s]), (pl.ds(BS, BS), second), (pl.ds(2 * BS, 2 * BS), -slot[s * BS:(s + 1) * BS])
        ):
            small[pl.ds(4 * s, 4), :, :, lanes] = value.reshape(4, 2, 16, value.shape[1])
    theirs = small.at[:, 1 - k]
    push(theirs, core, hs.at[0], hr.at[0], partner)

    def crossed(w, i, d, device):
        arrived(bx.at[w], gs.at[w], gr.at[w])
        bsum[i] = x_ref[rows_of(xl, d), lane_b] + bx[w]
        push(bsum.at[i], byin.at[i], es.at[i], er.at[i], device)

    arrived(core, hs.at[0], hr.at[0])
    mine[...] = small[:, k] + core[...]
    for d in range(1, 8):
        to = (r + d) % 8
        push(mine.at[to], rows_in.at[d - 1], us.at[d], ur.at[d], (to, c))
    crossed(0, 2, yfar, dfar)
    crossed(1, 0, yright, dr)
    crossed(2, 1, yleft, dl)
    total = mine[r]
    for d in range(1, 8):
        arrived(rows_in.at[d - 1], us.at[d], ur.at[d])
        total = total + rows_in[d - 1]
    parts[cc] = total
    for d in range(1, 8):
        push(parts.at[cc], parts.at[cc], ss.at[d], sr.at[d], (r, ((cc + d) % 8) * 2 + k))
    fin[...] = collect(q, 0)
    push(fin, yx, xs.at[5], xr.at[5], px)

    arrived(ax.at[3], xs.at[3], xr.at[3])
    first = x_ref[rows_of(xl, y), lane_a] + ax[3]
    arrived(al, rs.at[4, 2], rr.at[4, 2])
    arrived(ar, rs.at[4, 3], rr.at[4, 3])
    out[0, :, lane_a] = first + (al[...] + ar[...])

    own_half = pl.ds(pl.multiple_of(16 * k, 16), 16)
    for d in range(1, 8):
        arrived(parts.at[(cc + 8 - d) % 8], ss.at[d], sr.at[d])
    total = parts[0]
    for d in range(1, 8):
        total = total + parts[d]
    done[own_half, :] = total
    push(done.at[own_half], done.at[own_half], hs.at[1], hr.at[1], partner)

    lane_d = pl.ds(CROSS, COLS - CROSS)
    lane_e = pl.ds(COLS, BS)
    out[1, :, lane_d] = collect(xl, 1)
    arrived(bx.at[3], gs.at[3], gr.at[3])
    second = x_ref[rows_of(xl, y), lane_b] + bx[3]
    arrived(yx, xs.at[5], xr.at[5])
    out[1, :, lane_d] = out[1, :, lane_d] + yx[...]
    for i in range(3):
        arrived(byin.at[i], es.at[i], er.at[i])
    out[1, :, pl.ds(0, CROSS)] = (second + byin[0]) + (byin[1] + byin[2])
    other_half = pl.ds(pl.multiple_of(16 * (1 - k), 16), 16)
    arrived(done.at[other_half], hs.at[1], hr.at[1])
    out[0, :, lane_e] = done[:, pl.ds(0, BS)]
    out[1, :, lane_e] = done[:, pl.ds(BS, BS)]
    at_end = jnp.where(c == 15, 1.0, 0.0).astype(F32)
    tail = pl.ds(COLS - 2 * BS, 2 * BS)
    out[1, :, tail] = out[1, :, tail] + at_end * done[:, pl.ds(2 * BS, 2 * BS)]
    for copy in sent:
        copy.wait_send()

    @pl.when(r == 7)
    def _():
        for d in range(7):
            remote(last, own_q, qs.at[d], qr.at[0], (d, c)).wait_send()

    @pl.when(off_diagonal)
    def _():
        for level in range(2):
            for h in range(2):
                across(level, h).wait_send()

    @pl.when(diagonal)
    def _():
        for level in range(2):
            across_chip(level).wait_send()


def part_kernel(both_ref, panels, diagonals):
    panels[...] = both_ref[:, :, pl.ds(0, COLS)]
    diagonals[...] = both_ref[:, :, pl.ds(COLS, BS)]


def local(window, pattern, row_lists, factor, diag_inverse):
    dma = pltpu.SemaphoreType.DMA
    hbm = pl.BlockSpec(memory_space=pl.ANY)
    vmem = pl.BlockSpec(memory_space=pltpu.VMEM)
    smem = pl.BlockSpec(memory_space=pltpu.SMEM)
    v = lambda *shape: pltpu.VMEM(shape, F32)
    h = lambda *shape: pltpu.VMEM(shape, BF16)
    both_levels = pl.pallas_call(
        kernel,
        out_shape=jax.ShapeDtypeStruct((2, 32, COLS + BS), F32),
        in_specs=[vmem, smem, hbm, hbm, vmem],
        out_specs=vmem,
        scratch_shapes=[
            v(2, 16, 16, ROWS), v(2, 8, 2, 16, COLS), v(8, 2, 16, 2 * BS), v(ROWS, COLS), h(ROWS, COLS), h(ROWS, COLS),
            h(256, ROWS), h(256, ROWS), v(2, 2, ROWS), v(2, 2, COLS), v(256, 2 * COLS), v(256, COLS),
            h(256, COLS), h(256, COLS), h(256, COLS), h(256, COLS), h(256, COLS), h(256, COLS), v(256, 256),
            v(4, 32, COLS), v(3, 32, COLS), v(32, COLS), v(32, COLS), v(16, COLS), v(16, COLS),
            v(2, 3, 32, COLS - CROSS), v(32, COLS - CROSS), v(32, COLS - CROSS), v(4, 32, CROSS), v(3, 32, CROSS), v(3, 32, CROSS),
            v(8, 2, 16, SMALL), v(8, 16, SMALL), v(8, 16, SMALL), v(7, 16, SMALL), v(8, 16, SMALL), v(32, SMALL),
            dma((2, 9)), dma((2, 9)), dma((2, 9)), dma((2, 9)), dma((2, 8)), dma((2, 8)), dma((2, 2)), dma((2, 2)),
            dma((15,)), dma((8,)), dma((1,)), dma((1,)), dma((RB // 2,)), dma((6,)),
            dma((6,)), dma((6,)), dma((5, 4)), dma((5, 4)), dma((8,)), dma((8,)), dma((2,)), dma((2,)),
            dma((4,)), dma((4,)), dma((3,)), dma((3,)), dma((8,)), dma((8,)),
        ],
        compiler_params=pltpu.CompilerParams(
            collective_id=0, has_side_effects=True, vmem_limit_bytes=63 * 1024 * 1024
        ),
        name="selected_inversion",
    )(row_lists, jnp.swapaxes(pattern, 0, 1), window, jnp.swapaxes(factor, 1, 2), diag_inverse)
    panels, diagonals = pl.pallas_call(
        part_kernel,
        out_shape=(jax.ShapeDtypeStruct((2, 32, COLS), F32), jax.ShapeDtypeStruct((2, 32, BS), F32)),
        in_specs=[vmem],
        out_specs=(vmem, vmem),
        name="parts",
    )(both_levels)
    return jnp.swapaxes(panels, 1, 2), jnp.swapaxes(diagonals, 1, 2)


def solution(mesh):
    in_specs = (P("prow", "pcol"), P("prow", "pcol"), P(), P(None, "prow", "pcol"), P())
    out_specs = (P(None, "pcol", "prow"), P(None, None, "prow"))
    return jax.shard_map(local, mesh=mesh, in_specs=in_specs, out_specs=out_specs, check_vma=False)
```
